32 devices in a mesh: groups: 2 (over y), roll: 4 (over z), tp: 2 (over x), seq: 2 (over core).
Axes of the slice: x: 2, y: 2, z: 4, core: 2. Of those that a mesh axis runs over, the one named last changes fastest.
Arguments:
- hidden: bfloat16 [128, 8192], P('groups', ('roll', 'seq')), parts along dimension 0, may hold values from -6 to 6
- w_query: bfloat16 [8192, 8192], P(('roll', 'seq'), 'tp'), may hold values from -0.0625 to 0.0625
- w_key: bfloat16 [8192, 1024], P(('roll', 'seq'), 'tp'), may hold values from -0.0625 to 0.0625
- w_value: bfloat16 [8192, 1024], P(('roll', 'seq'), 'tp'), may hold values from -0.0625 to 0.0625
- b_query: bfloat16 [8192], P('tp'), may hold values from -12 to 12
- b_key: bfloat16 [1024], P('tp'), may hold values from -12 to 12
- b_value: bfloat16 [1024], P('tp'), may hold values from -6 to 6
- w_out: bfloat16 [8192, 8192], P('tp', ('roll', 'seq')), may hold values from -0.0625 to 0.0625
- prefix_keys: bfloat16 [4, 4096, 1024], P('groups', ('roll', 'seq'), 'tp'), parts along dimension 0, may hold values from -256 to 256
- prefix_values: bfloat16 [4, 4096, 1024], P('groups', ('roll', 'seq'), 'tp'), parts along dimension 0, may hold values from -6 to 6
- suffix_keys: bfloat16 [16, 2048, 1024], P(('groups', 'roll'), 'seq', 'tp'), parts along dimension 0, may hold values from -6 to 6
- suffix_values: bfloat16 [16, 2048, 1024], P(('groups', 'roll'), 'seq', 'tp'), parts along dimension 0, may hold values from -6 to 6
- suffix_lengths: int32 [16], P('groups'), parts along dimension 0, may hold values from 1 to 2048, 8192 in all
- prompt_of: int32 [16], P('groups'), parts along dimension 0, may hold values from 0 to 1, as said below
Outputs:
- attended: bfloat16 [128, 8192], P(('groups', 'tp'), ('roll', 'seq')), parts along dimension 0
The draws below stay inside these ranges and needn't reach their ends.
There are 2 independent parts, one for each index of `groups`. The reference program is written for one: setup_inputs(seed, part) draws one part's arguments, and reference() takes and returns one part's arrays. A program takes and returns all parts, laid end to end along the dimension named above; an argument that names none is the same for every part. Nothing has to cross between parts.
Inputs may be any that keep to these rules, and one draw needn't show every extreme that they name: Only the first suffix_lengths[r] rows of a rollout's suffix cache are live; the lengths of a group add up to 8192 and the largest is exactly 2048. `prompt_of`: every prompt is extended by exactly 4 rollouts.
All inputs are finite; a program needn't handle non-finite values.
Results may differ from the reference program's by a relative error of at most 0.009.
The reference program's roundings to bfloat16 on the way (of `query`, `key_new`, `value_new` and `attention`) count: a program that leaves them out, or rounds other values in their place, can miss the bound.
Values may be sent and summed in bfloat16 or wider, within the bound.
No kernel may reach another device: no remote copies, remote signals or barrier semaphores. Data moves between devices by JAX's collectives and lax.ppermute only.
A program may use at most 128 MiB of HBM per device.

```python
import math
import jax
import jax.numpy as jnp
import numpy as np
from jax import lax

D = 8192
H = 64
KVH = 8
HD = 128
PROMPTS = 2
GUESS = 8
PREFIX = 4096
ROLLOUTS = 8
SUFFIX = 2048
TOKENS = 64


def draw_prefix_keys(key, part):
    base = jnp.clip(jax.random.normal(key, (PROMPTS, PREFIX, KVH * HD), jnp.float32), -8.0, 8.0)
    return base.astype(jnp.bfloat16)


def draw_prompt_of(key, part):
    return (jax.random.permutation(key, ROLLOUTS) % PROMPTS).astype(jnp.int32)


def block_scale(rng, dims, shards, least, top_value):
    loudness, own = 1.0, jax.random.fold_in(rng, 6)
    for axis_at, shards_of in shards:
        steps = jnp.exp(jax.random.uniform(jax.random.fold_in(own, axis_at), (shards_of,), jnp.float32, least / len(shards), top_value / len(shards)))
        loudness = loudness * jnp.repeat(steps, dims[axis_at] // shards_of).reshape([-1 if axis == axis_at else 1 for axis in range(len(dims))])
    return loudness


def profile(number_of, total, bound, lean):
    loads = [(1 << 20) // math.isqrt(rank ** lean) + 1 for rank in range(2, number_of + 1)]
    spare, counts = total - bound - (number_of - 1), [1] * (number_of - 1)
    while spare > 0:
        movable = [i for i in range(number_of - 1) if counts[i] < bound]
        pool, budget = sum([loads[i] for i in movable]), spare
        for i in movable:
            extra = min(bound - counts[i], max(1, budget * loads[i] // pool), spare)
            counts[i] = counts[i] + extra
            spare = spare - extra
    return np.array([bound] + counts)


def uneven_parts(key, number_of, total, bound, slope):
    if number_of == 2:
        one = jax.random.randint(key, (), max(1, total - bound), min(bound, total - 1) + 1)
        return jnp.stack([one, total - one])
    lengths = jnp.asarray(profile(number_of, total, bound, slope), jnp.int32)
    pairs = (number_of - 1) // 2
    giver, receiver = lengths[1:1 + 2 * pairs:2], lengths[2:2 + 2 * pairs:2]
    slack = jnp.minimum(giver - 1, bound - receiver)
    passed = jax.random.randint(jax.random.fold_in(key, 1), (pairs,), 0, 1 << 20) % (slack + 1)
    lengths = lengths.at[1:1 + 2 * pairs:2].set(giver - passed).at[2:2 + 2 * pairs:2].set(receiver + passed)
    return lengths[jax.random.permutation(jax.random.fold_in(key, 2), number_of)]


def scatter_about(rng, shape, deviation, bound, pieces=(), held_as=jnp.bfloat16):
    values = jax.random.normal(rng, shape, jnp.float32) * deviation
    if len(pieces) > 0:
        values = block_scale(rng, shape, pieces, -0.22, 0.18) * values
    return jnp.clip(values, min=-bound, max=bound).astype(held_as)


def setup_inputs(seed: int = 0, part: int = 0) -> dict:
    arg_keys = jax.random.split(jax.random.key(seed), 15)
    own_keys = jax.random.split(jax.random.fold_in(arg_keys[14], part), 15)
    hidden = scatter_about(own_keys[0], (TOKENS, D), 1.0, 6.0, ((1, 8),))
    w_query = scatter_about(arg_keys[1], (D, H * HD), D ** -0.5, 0.0625, ((0, 8), (1, 2)))
    w_key = scatter_about(arg_keys[2], (D, KVH * HD), D ** -0.5, 0.0625, ((0, 8), (1, 2)))
    w_value = scatter_about(arg_keys[3], (D, KVH * HD), D ** -0.5, 0.0625, ((0, 8), (1, 2)))
    b_query = scatter_about(arg_keys[4], (H * HD,), 3.0, 12.0, ((0, 2),))
    b_key = scatter_about(arg_keys[5], (KVH * HD,), 3.0, 12.0, ((0, 2),))
    b_value = scatter_about(arg_keys[6], (KVH * HD,), 1.0, 6.0, ((0, 2),))
    w_out = scatter_about(arg_keys[7], (H * HD, D), (H * HD) ** -0.5, 0.0625, ((0, 2), (1, 8)))
    prefix_keys = draw_prefix_keys(jax.random.fold_in(jax.random.fold_in(arg_keys[14], part), 71), part)
    prefix_values = scatter_about(own_keys[9], (PROMPTS, PREFIX, KVH * HD), 1.0, 6.0, ((1, 8), (2, 2)))
    suffix_keys = scatter_about(own_keys[10], (ROLLOUTS, SUFFIX, KVH * HD), 1.0, 6.0, ((0, 4), (1, 2), (2, 2)))
    suffix_values = scatter_about(own_keys[11], (ROLLOUTS, SUFFIX, KVH * HD), 1.0, 6.0, ((0, 4), (1, 2), (2, 2)))
    suffix_lengths = uneven_parts(own_keys[12], ROLLOUTS, ROLLOUTS * SUFFIX // 2, SUFFIX, 2).astype(jnp.int32)
    prompt_of = draw_prompt_of(jax.random.fold_in(jax.random.fold_in(arg_keys[14], part), 71), part)
    return dict(hidden=hidden, w_query=w_query, w_key=w_key, w_value=w_value, b_query=b_query, b_key=b_key, b_value=b_value, w_out=w_out, prefix_keys=prefix_keys, prefix_values=prefix_values, suffix_keys=suffix_keys, suffix_values=suffix_values, suffix_lengths=suffix_lengths, prompt_of=prompt_of)


ROPE_BASE = 1000000.0

def rotate(values, positions):
    half = values.shape[-1] // 2
    steps = jnp.arange(half).astype(jnp.float32) * (2.0 / values.shape[-1])
    freqs = jnp.exp(-math.log(ROPE_BASE) * steps)
    angles = positions[:, None] * freqs[None, :]
    cosine = jnp.cos(angles)[:, None, :]
    sine = jnp.sin(angles)[:, None, :]
    first = values[..., :half]
    second = values[..., half:]
    return jnp.concatenate([first * cosine - second * sine, second * cosine + first * sine], axis=-1)

def project(hidden, weight, bias):
    return jnp.dot(hidden, weight, preferred_element_type=jnp.float32) + bias.astype(jnp.float32)

def reference(hidden, w_query, w_key, w_value, b_query, b_key, b_value, w_out, prefix_keys, prefix_values, suffix_keys, suffix_values, suffix_lengths, prompt_of):
    row_count = hidden.shape[0]
    group = H // KVH
    row_ids = jnp.arange(row_count, dtype=jnp.int32)
    owners = row_ids // GUESS
    offsets = row_ids % GUESS
    positions = (PREFIX + suffix_lengths[owners] + offsets).astype(jnp.float32)
    query = rotate(project(hidden, w_query, b_query).reshape(row_count, H, HD), positions).astype(jnp.bfloat16)
    key_new = rotate(project(hidden, w_key, b_key).reshape(row_count, KVH, HD), positions).astype(jnp.bfloat16)
    value_new = project(hidden, w_value, b_value).astype(jnp.bfloat16).reshape(row_count, KVH, HD)
    scale = 1.0 / math.sqrt(HD)
    key_ids = jnp.arange(PREFIX + SUFFIX + GUESS, dtype=jnp.int32)
    guess_ids = jnp.arange(GUESS, dtype=jnp.int32)

    def one_rollout(rollout):
        start = (rollout * GUESS).astype(jnp.int32)
        prompt = prompt_of[rollout].astype(jnp.int32)
        queries = lax.dynamic_slice_in_dim(query, start, GUESS, 0).astype(jnp.float32).reshape(GUESS, KVH, group, HD)
        keys = jnp.concatenate([lax.dynamic_index_in_dim(prefix_keys, prompt, 0, keepdims=False).astype(jnp.float32).reshape(PREFIX, KVH, HD), lax.dynamic_index_in_dim(suffix_keys, rollout, 0, keepdims=False).astype(jnp.float32).reshape(SUFFIX, KVH, HD), lax.dynamic_slice_in_dim(key_new, start, GUESS, 0).astype(jnp.float32)], axis=0)
        values = jnp.concatenate([lax.dynamic_index_in_dim(prefix_values, prompt, 0, keepdims=False).astype(jnp.float32).reshape(PREFIX, KVH, HD), lax.dynamic_index_in_dim(suffix_values, rollout, 0, keepdims=False).astype(jnp.float32).reshape(SUFFIX, KVH, HD), lax.dynamic_slice_in_dim(value_new, start, GUESS, 0).astype(jnp.float32)], axis=0)
        length = suffix_lengths[rollout]
        in_suffix = key_ids - PREFIX < length
        in_guess = key_ids[None, :] - (PREFIX + SUFFIX) <= guess_ids[:, None]
        visible = jnp.where((key_ids < PREFIX)[None, :], True, jnp.where((key_ids < PREFIX + SUFFIX)[None, :], in_suffix[None, :], in_guess))
        scores = jnp.einsum('tkgd,skd->tkgs', queries, keys) * scale
        scores = jnp.where(visible[:, None, None, :], scores, -jnp.inf)
        peak = lax.optimization_barrier(jnp.max(scores, axis=-1))
        weights = jnp.exp(scores - peak[..., None])
        total = lax.optimization_barrier(jnp.sum(weights, axis=-1))
        rounded = lax.optimization_barrier(weights.astype(jnp.bfloat16)).astype(jnp.float32)
        output = jnp.einsum('tkgs,skd->tkgd', rounded, values) / total[..., None]
        return output.reshape(GUESS, H * HD)
    attention = lax.map(one_rollout, jnp.arange(ROLLOUTS, dtype=jnp.int32))
    attention = attention.reshape(row_count, H * HD).astype(jnp.bfloat16)
    return jnp.dot(attention, w_out, preferred_element_type=jnp.float32).astype(jnp.bfloat16)
```

```python
import functools
import math

import jax
import jax.numpy as jnp
from jax import lax
from jax.experimental import pallas as pl
from jax.experimental.pallas import tpu as pltpu
from jax.sharding import PartitionSpec as P

HD = 128
GUESS = 8


ROPE_BASE = 1000000.0
NEG_FILL = -1e30


def rotate(values, positions):
    half = values.shape[-1] // 2
    steps = jnp.arange(half).astype(jnp.float32) * (2.0 / values.shape[-1])
    freqs = jnp.exp(-math.log(ROPE_BASE) * steps)
    angles = positions[:, None] * freqs[None, :]
    cosine = jnp.cos(angles)[:, None, :]
    sine = jnp.sin(angles)[:, None, :]
    first = values[..., :half]
    second = values[..., half:]
    return jnp.concatenate(
        [first * cosine - second * sine, second * cosine + first * sine], axis=-1
    )


def lookup(table, indices):
    hits = indices[:, None] == jnp.arange(table.shape[0], dtype=jnp.int32)[None, :]
    return jnp.sum(jnp.where(hits, table[None, :], 0), axis=1)


def combine(first, second):
    peak_a, total_a, numer_a = first
    peak_b, total_b, numer_b = second
    peak = jnp.maximum(peak_a, peak_b)
    factor_a = jnp.exp(peak_a - peak)
    factor_b = jnp.exp(peak_b - peak)
    return (
        peak,
        total_a * factor_a + total_b * factor_b,
        numer_a * factor_a[..., None] + numer_b * factor_b[..., None],
    )


def masked_stats(scores, visible, values):
    peak = jnp.max(jnp.where(visible, scores, NEG_FILL), axis=-1)
    weights = jnp.exp(jnp.where(visible, scores - peak[..., None], NEG_FILL))
    total = jnp.sum(weights, axis=-1)
    numer = jnp.einsum(
        "rtkgs,rskd->rtkgd",
        weights.astype(jnp.bfloat16),
        values,
        preferred_element_type=jnp.float32,
    )
    return (peak, total, numer)


def general_body(
    hidden,
    w_query,
    w_key,
    w_value,
    b_query,
    b_key,
    b_value,
    w_out,
    prefix_keys,
    prefix_values,
    suffix_keys,
    suffix_values,
    suffix_lengths,
    prompt_of,
):
    row_count = hidden.shape[0]
    q_heads = w_query.shape[1] // HD
    kv_heads = w_key.shape[1] // HD
    group = q_heads // kv_heads
    prompts = prefix_keys.shape[0]
    pre_dev = prefix_keys.shape[1]
    prefix_total = pre_dev * lax.axis_size(("roll", "seq"))
    per_device = suffix_keys.shape[0]
    suf_dev = suffix_keys.shape[1]
    scale = 1.0 / math.sqrt(HD)
    q_part = jnp.dot(hidden, w_query, preferred_element_type=jnp.float32)
    k_part = jnp.dot(hidden, w_key, preferred_element_type=jnp.float32)
    v_part = jnp.dot(hidden, w_value, preferred_element_type=jnp.float32)
    q_sum, k_sum, v_sum = lax.psum((q_part, k_part, v_part), ("roll", "seq"))
    count = q_sum.shape[0]
    row_ids = jnp.arange(count, dtype=jnp.int32)
    owner_ids = row_ids // GUESS
    positions = (prefix_total + lookup(suffix_lengths, owner_ids) + row_ids % GUESS).astype(
        jnp.float32
    )
    q_rot = rotate((q_sum + b_query.astype(jnp.float32)).reshape(count, q_heads, HD), positions)
    k_rot = rotate((k_sum + b_key.astype(jnp.float32)).reshape(count, kv_heads, HD), positions)
    v_fin = (v_sum + b_value.astype(jnp.float32)).reshape(count, kv_heads, HD)
    query = q_rot.astype(jnp.bfloat16)
    key_new = k_rot.astype(jnp.bfloat16)
    value_new = v_fin.astype(jnp.bfloat16)
    query_grid = query.reshape(row_count, kv_heads, group, HD)
    owners_all = jnp.arange(row_count, dtype=jnp.int32) // GUESS
    row_prompt = lookup(prompt_of, owners_all)
    pre_keys = prefix_keys.reshape(prompts, pre_dev, kv_heads, HD)
    pre_values = prefix_values.reshape(prompts, pre_dev, kv_heads, HD)
    peak_all = jnp.full((row_count, kv_heads, group), NEG_FILL, jnp.float32)
    total_all = jnp.zeros((row_count, kv_heads, group), jnp.float32)
    numer_all = jnp.zeros((row_count, kv_heads, group, HD), jnp.float32)
    for prompt in range(prompts):
        scores = (
            jnp.einsum(
                "tkgd,skd->tkgs", query_grid, pre_keys[prompt], preferred_element_type=jnp.float32
            )
            * scale
        )
        block_peak = jnp.max(scores, axis=-1)
        weights = jnp.exp(scores - block_peak[..., None])
        block_numer = jnp.einsum(
            "tkgs,skd->tkgd",
            weights.astype(jnp.bfloat16),
            pre_values[prompt],
            preferred_element_type=jnp.float32,
        )
        picked = (row_prompt == prompt)[:, None, None]
        peak_all = jnp.where(picked, block_peak, peak_all)
        total_all = jnp.where(picked, jnp.sum(weights, axis=-1), total_all)
        numer_all = jnp.where(picked[..., None], block_numer, numer_all)
    first_rollout = lax.axis_index("roll") * per_device
    seq_index = lax.axis_index("seq")
    local_len = lax.dynamic_slice_in_dim(suffix_lengths, first_rollout, per_device, 0)
    live = jnp.clip(local_len - seq_index * suf_dev, 0, suf_dev)
    row_start = first_rollout * GUESS
    local_rows = per_device * GUESS
    query_local = lax.dynamic_slice_in_dim(query_grid, row_start, local_rows, 0).reshape(
        per_device, GUESS, kv_heads, group, HD
    )
    suf_keys = suffix_keys.reshape(per_device, suf_dev, kv_heads, HD)
    suf_values = suffix_values.reshape(per_device, suf_dev, kv_heads, HD)
    scores = (
        jnp.einsum("rtkgd,rskd->rtkgs", query_local, suf_keys, preferred_element_type=jnp.float32)
        * scale
    )
    visible = (jnp.arange(suf_dev, dtype=jnp.int32)[None, :] < live[:, None])[
        :, None, None, None, :
    ]
    suffix_part = masked_stats(scores, visible, suf_values)
    key_local = lax.dynamic_slice_in_dim(key_new, row_start, local_rows, 0).reshape(
        per_device, GUESS, kv_heads, HD
    )
    value_local = lax.dynamic_slice_in_dim(value_new, row_start, local_rows, 0).reshape(
        per_device, GUESS, kv_heads, HD
    )
    new_scores = (
        jnp.einsum("rtkgd,rskd->rtkgs", query_local, key_local, preferred_element_type=jnp.float32)
        * scale
    )
    guess_ids = jnp.arange(GUESS, dtype=jnp.int32)
    causal = (guess_ids[None, :] <= guess_ids[:, None]) & (seq_index == 0)
    guess_part = masked_stats(new_scores, causal[None, :, None, None, :], value_local)
    prefix_local = (
        lax.dynamic_slice_in_dim(peak_all, row_start, local_rows, 0).reshape(
            per_device, GUESS, kv_heads, group
        ),
        lax.dynamic_slice_in_dim(total_all, row_start, local_rows, 0).reshape(
            per_device, GUESS, kv_heads, group
        ),
        lax.dynamic_slice_in_dim(numer_all, row_start, local_rows, 0).reshape(
            per_device, GUESS, kv_heads, group, HD
        ),
    )
    peak_loc, total_loc, numer_loc = combine(combine(prefix_local, suffix_part), guess_part)
    peak_all = lax.dynamic_update_slice_in_dim(
        peak_all, peak_loc.reshape(local_rows, kv_heads, group), row_start, 0
    )
    total_all = lax.dynamic_update_slice_in_dim(
        total_all, total_loc.reshape(local_rows, kv_heads, group), row_start, 0
    )
    numer_all = lax.dynamic_update_slice_in_dim(
        numer_all, numer_loc.reshape(local_rows, kv_heads, group, HD), row_start, 0
    )
    peaks, totals, numers = (
        lax.all_to_all(peak_all[None], ("roll", "seq"), split_axis=1, concat_axis=0, tiled=True),
        lax.all_to_all(total_all[None], ("roll", "seq"), split_axis=1, concat_axis=0, tiled=True),
        lax.all_to_all(numer_all[None], ("roll", "seq"), split_axis=1, concat_axis=0, tiled=True),
    )
    peak_top = jnp.max(peaks, axis=0)
    factors = jnp.exp(peaks - peak_top[None])
    share = (
        jnp.sum(numers * factors[..., None], axis=0) / jnp.sum(totals * factors, axis=0)[..., None]
    )
    share = share.astype(jnp.bfloat16).reshape(share.shape[0], q_heads * HD)
    attention = lax.all_gather(share, ("roll", "seq"), axis=0, tiled=True)
    summed = lax.psum_scatter(
        jnp.dot(attention, w_out, preferred_element_type=jnp.float32),
        "tp",
        scatter_dimension=0,
        tiled=True,
    )
    return summed.astype(jnp.bfloat16)


VMEM_ALL = 60 << 20


def contract_last(a, b):
    return lax.dot_general(a, b, (((1,), (1,)), ((), ())), preferred_element_type=jnp.float32)


def project_kernel(meta, x_ref, wq_ref, wk_ref, wv_ref, out_ref):
    zone = meta[0]
    roll = out_ref.shape[0]
    block = out_ref.shape[2]
    x = x_ref[...]
    at = 0
    for w_ref in (wq_ref, wk_ref, wv_ref):
        width = w_ref.shape[1]
        part = jnp.dot(x, w_ref[...], preferred_element_type=jnp.float32)
        for b in range(roll):
            out_ref[b ^ zone, 0, :, at : at + width] = part[b * block : (b + 1) * block]
        at += width


def project(meta, hidden, w_query, w_key, w_value, roll, kh, flip):
    rows, depth = hidden.shape
    kv_heads = w_key.shape[1] // HD
    wide = w_query.shape[1] // kv_heads
    block = rows // roll
    width = wide + 2 * HD

    def column(j, meta):
        half = 1 - meta[1] if flip else meta[1]
        return (0, half * kh + j)

    return pl.pallas_call(
        project_kernel,
        out_shape=jax.ShapeDtypeStruct((roll, kh, block, width), jnp.float32),
        grid_spec=pltpu.PrefetchScalarGridSpec(
            num_scalar_prefetch=1,
            grid=(kh,),
            in_specs=[
                pl.BlockSpec((rows, depth), lambda j, meta: (0, 0)),
                pl.BlockSpec((depth, wide), column),
                pl.BlockSpec((depth, HD), column),
                pl.BlockSpec((depth, HD), column),
            ],
            out_specs=pl.BlockSpec((roll, 1, block, width), lambda j, meta: (0, j, 0, 0)),
        ),
        compiler_params=pltpu.CompilerParams(vmem_limit_bytes=VMEM_ALL),
        cost_estimate=pl.CostEstimate(
            flops=2 * rows * depth * width * kh,
            bytes_accessed=2 * depth * width * kh + 4 * rows * width * kh,
            transcendentals=0,
        ),
        name="project_send" if flip else "project_keep",
    )(meta, hidden, w_query, w_key, w_value)


def finish_kernel(group, per, meta, keep_ref, got_ref, *refs):
    others = refs[:-8]
    bq_ref, bk_ref, bv_ref, cos_ref, sin_ref, q_ref, k_ref, v_ref = refs[-8:]
    kh = keep_ref.shape[1]
    guess = cos_ref.shape[0] // per
    cosine = cos_ref[...]
    sine = sin_ref[...]

    def total(j, g):
        at = slice(g * HD, (g + 1) * HD)
        u = keep_ref[0, j, :, at] + got_ref[0, j, :, at]
        for o in others:
            u = u + o[j, :, at]
        if g < group:
            bias = bq_ref[:, (j * group + g) * HD : (j * group + g + 1) * HD]
        else:
            bias = (bk_ref if g == group else bv_ref)[:, j * HD : (j + 1) * HD]
        return u + bias.astype(jnp.float32)

    def turn(u):
        return u * cosine + pltpu.roll(u, HD // 2, 1) * sine

    for j in range(kh):
        for g in range(0, group, 2):
            one = turn(total(j, g))
            two = turn(total(j, g + 1))
            for i in range(per):
                span = slice(i * guess, (i + 1) * guess)
                both = jnp.concatenate([one[span], two[span]], axis=0)
                q_ref[i, j, g * guess : (g + 2) * guess, :] = both.astype(jnp.bfloat16)
        k_ref[j] = turn(total(j, group)).astype(jnp.bfloat16)
        v_ref[j] = total(j, group + 1).astype(jnp.bfloat16)


def finish(meta, keep, got, others, biases, cosine, sine, per):
    roll, kh, block, width = keep.shape
    group = width // HD - 2
    guess = block // per
    first = pl.BlockSpec((1, kh, block, width), lambda n, meta: (0, 0, 0, 0))
    part = pl.BlockSpec((kh, block, width), lambda n, meta: (0, 0, 0))
    table = pl.BlockSpec((block, HD), lambda n, meta: (meta[0], 0))

    def half(bias):
        return pl.BlockSpec((1, bias.shape[1] // 2), lambda n, meta: (0, meta[1]))

    return pl.pallas_call(
        functools.partial(finish_kernel, group, per),
        grid_spec=pltpu.PrefetchScalarGridSpec(
            num_scalar_prefetch=1,
            grid=(1,),
            in_specs=[first, first] + [part] * len(others) + [half(b) for b in biases] + [table, table],
            out_specs=(
                pl.BlockSpec((per, kh, group * guess, HD), lambda n, meta: (0, 0, 0, 0)),
                pl.BlockSpec((kh, block, HD), lambda n, meta: (0, 0, 0)),
                pl.BlockSpec((kh, block, HD), lambda n, meta: (0, 0, 0)),
            ),
        ),
        out_shape=(
            jax.ShapeDtypeStruct((per, kh, group * guess, HD), jnp.bfloat16),
            jax.ShapeDtypeStruct((kh, block, HD), jnp.bfloat16),
            jax.ShapeDtypeStruct((kh, block, HD), jnp.bfloat16),
        ),
        compiler_params=pltpu.CompilerParams(vmem_limit_bytes=16 << 20),
        name="finish",
    )(meta, keep, got, *others, *biases, cosine, sine)


def own_kernel(scale, guess, meta, lengths, q_ref, kn_ref, vn_ref, k0_ref, k1_ref, v0_ref, v1_ref, n_ref, m_ref, l_ref):
    per, kh, width, _ = q_ref.shape
    span = k0_ref.shape[1]
    seq = meta[1]
    fresh = kn_ref.shape[1]
    key_id = lax.broadcasted_iota(jnp.int32, (width, span), 1)
    new_id = lax.broadcasted_iota(jnp.int32, (width, fresh), 1)
    row_id = lax.broadcasted_iota(jnp.int32, (width, fresh), 0) % guess
    for i in range(per):
        length = lengths[meta[0] * per + i]
        sees = (key_id < length - seq * span, key_id < length - (1 - seq) * span)
        causal = (new_id >= i * guess) & (new_id - i * guess <= row_id)
        sees = sees + (causal,)
        for j in range(kh):
            q = q_ref[i, j]
            at = slice(j * HD, (j + 1) * HD)
            keys = (k0_ref[i, :, at], k1_ref[i, :, at], kn_ref[j])
            values = (v0_ref[i, :, at], v1_ref[i, :, at], vn_ref[j])
            scores = [jnp.where(see, contract_last(q, k) * scale, NEG_FILL) for k, see in zip(keys, sees)]
            peak = jnp.max(scores[0], axis=1, keepdims=True)
            for s in scores[1:]:
                peak = jnp.maximum(peak, jnp.max(s, axis=1, keepdims=True))
            total = jnp.zeros((width, 1), jnp.float32)
            numer = jnp.zeros((width, HD), jnp.float32)
            for s, v in zip(scores, values):
                w = jnp.exp(s - peak)
                total = total + jnp.sum(w, axis=1, keepdims=True)
                numer = numer + jnp.dot(w.astype(jnp.bfloat16), v, preferred_element_type=jnp.float32)
            n_ref[i, j] = numer
            m_ref[i, j] = jnp.broadcast_to(peak, (width, HD))
            l_ref[i, j] = jnp.broadcast_to(total, (width, HD))


def own_attention(meta, lengths, q, k_new, v_new, keys, keys_got, values, values_got, scale, guess):
    per, kh, width, _ = q.shape
    span = keys.shape[1]
    cols = kh * HD
    local = pl.BlockSpec((per, span, cols), lambda n, meta, lengths: (0, 0, meta[1]))
    got = pl.BlockSpec((per, span, cols), lambda n, meta, lengths: (0, 0, 0))
    fresh = pl.BlockSpec(k_new.shape, lambda n, meta, lengths: (0, 0, 0))
    whole = pl.BlockSpec(q.shape, lambda n, meta, lengths: (0, 0, 0, 0))
    out = jax.ShapeDtypeStruct(q.shape, jnp.float32)
    elements = per * kh * width * span * 2
    return pl.pallas_call(
        functools.partial(own_kernel, scale, guess),
        grid_spec=pltpu.PrefetchScalarGridSpec(
            num_scalar_prefetch=2,
            grid=(1,),
            in_specs=[whole, fresh, fresh, local, got, local, got],
            out_specs=(whole, whole, whole),
        ),
        out_shape=(out, out, out),
        compiler_params=pltpu.CompilerParams(vmem_limit_bytes=24 << 20),
        cost_estimate=pl.CostEstimate(
            flops=4 * elements * HD, bytes_accessed=8 * per * span * cols, transcendentals=elements
        ),
        name="own_attention",
    )(meta, lengths, q, k_new, v_new, keys, keys_got, values, values_got)


def split_three(x):
    high = x.astype(jnp.bfloat16).astype(jnp.float32)
    rest = x - high
    middle = rest.astype(jnp.bfloat16).astype(jnp.float32)
    return high, middle, rest - middle


def prefix_kernel(scale, roll, meta, prompts, *refs):
    q_refs = refs[:roll]
    k0_ref, k1_ref, v0_ref, v1_ref, on_ref, om_ref, ol_ref = refs[roll : roll + 7]
    n_out, m_out, l_out = refs[roll + 7 : roll + 10]
    packed = refs[roll + 10 : 2 * roll + 9]
    q_all, n_all, m_all, l_all, order = refs[2 * roll + 9 :]
    per, kh, width, _ = q_refs[0].shape
    prompt = pl.program_id(0)
    j = pl.program_id(1)
    share = roll * per // pl.num_programs(0)

    @pl.when((prompt == 0) & (j == 0))
    def _():
        for k in range(roll):
            q_all[k * per : (k + 1) * per] = q_refs[k][...]

    @pl.when(j == 0)
    def _():
        filled = jnp.int32(0)
        for k in range(roll):
            for i in range(per):
                chosen = prompts[(meta[0] ^ k) * per + i] == prompt

                @pl.when(chosen)
                def _():
                    order[filled] = k * per + i

                filled = filled + chosen.astype(jnp.int32)

    ids = [order[n] for n in range(share)]
    q = jnp.concatenate([q_all[at, j] for at in ids], axis=0)
    scores = [contract_last(q, k_ref[0]) * scale for k_ref in (k0_ref, k1_ref)]
    peak = jnp.maximum(
        jnp.max(scores[0], axis=1, keepdims=True), jnp.max(scores[1], axis=1, keepdims=True)
    )
    total = jnp.zeros(peak.shape, jnp.float32)
    numer = jnp.zeros((share * width, HD), jnp.float32)
    for s, v_ref in zip(scores, (v0_ref, v1_ref)):
        w = jnp.exp(s - peak)
        total = total + jnp.sum(w, axis=1, keepdims=True)
        numer = numer + jnp.dot(w.astype(jnp.bfloat16), v_ref[0], preferred_element_type=jnp.float32)
    peak = jnp.broadcast_to(peak, numer.shape)
    total = jnp.broadcast_to(total, numer.shape)
    for n, at in enumerate(ids):
        span = slice(n * width, (n + 1) * width)
        n_all[at, j] = numer[span]
        m_all[at, j] = peak[span]
        l_all[at, j] = total[span]

    @pl.when((prompt == pl.num_programs(0) - 1) & (j == kh - 1))
    def _():
        for i in range(per):
            for h in range(kh):
                m_a, m_b = m_all[i, h], om_ref[i, h]
                peak = jnp.maximum(m_a, m_b)
                f_a, f_b = jnp.exp(m_a - peak), jnp.exp(m_b - peak)
                m_out[i, h] = peak
                l_out[i, h] = l_all[i, h] * f_a + ol_ref[i, h] * f_b
                n_out[i, h] = n_all[i, h] * f_a + on_ref[i, h] * f_b
        lane = lax.broadcasted_iota(jnp.int32, (width, HD), 1)
        for k in range(1, roll):
            stats = jnp.zeros((width, HD), jnp.float32)
            for i in range(per):
                for h in range(kh):
                    u = i * kh + h
                    packed[k - 1][u * width : (u + 1) * width, :] = n_all[k * per + i, h].astype(jnp.bfloat16)
                    pieces = split_three(m_all[k * per + i, h]) + split_three(l_all[k * per + i, h])
                    for c, piece in enumerate(pieces):
                        stats = jnp.where(lane == 6 * u + c, piece, stats)
            u = per * kh
            packed[k - 1][u * width : (u + 1) * width, :] = stats.astype(jnp.bfloat16)


def prefix_attention(meta, prompt_of, queries, keys, keys_got, values, values_got, own, scale):
    roll = len(queries)
    per, kh, width, _ = queries[0].shape
    prompts, span, _ = keys.shape
    local = pl.BlockSpec((1, span, HD), lambda p, j, meta, prompts: (p, 0, meta[1] * kh + j))
    got = pl.BlockSpec((1, span, HD), lambda p, j, meta, prompts: (p, 0, j))
    whole = pl.BlockSpec(queries[0].shape, lambda p, j, meta, prompts: (0, 0, 0, 0))
    rows = (per * kh + 1) * width
    sent = pl.BlockSpec((rows, HD), lambda p, j, meta, prompts: (0, 0))
    out = jax.ShapeDtypeStruct(queries[0].shape, jnp.float32)
    elements = roll * per * kh * width * span * 2
    everything = (roll * per, kh, width, HD)
    outs = pl.pallas_call(
        functools.partial(prefix_kernel, scale, roll),
        grid_spec=pltpu.PrefetchScalarGridSpec(
            num_scalar_prefetch=2,
            grid=(prompts, kh),
            in_specs=[whole] * roll + [local, got, local, got] + [whole] * 3,
            out_specs=[whole] * 3 + [sent] * (roll - 1),
            scratch_shapes=[pltpu.VMEM(everything, jnp.bfloat16)] + [pltpu.VMEM(everything, jnp.float32)] * 3
            + [pltpu.SMEM((roll * per,), jnp.int32)],
        ),
        out_shape=[out] * 3 + [jax.ShapeDtypeStruct((rows, HD), jnp.bfloat16)] * (roll - 1),
        compiler_params=pltpu.CompilerParams(vmem_limit_bytes=24 << 20),
        cost_estimate=pl.CostEstimate(
            flops=4 * elements * HD, bytes_accessed=8 * prompts * span * kh * HD, transcendentals=elements
        ),
        name="prefix_attention",
    )(meta, prompt_of, *queries, keys, keys_got, values, values_got, *own)
    return outs[:3], outs[3:]


def merge_kernel(group, n_ref, m_ref, l_ref, *refs):
    packed, out_ref = refs[:-1], refs[-1]
    per, kh, width, _ = n_ref.shape
    guess = width // group
    stats = [p[per * kh * width :, :].astype(jnp.float32) for p in packed]
    results = {}
    for i in range(per):
        for h in range(kh):
            u = i * kh + h

            def column(s, c):
                c = 6 * u + c
                return s[:, c : c + 1] + s[:, c + 1 : c + 2] + s[:, c + 2 : c + 3]

            peaks = [m_ref[i, h]] + [jnp.broadcast_to(column(s, 0), (width, HD)) for s in stats]
            totals = [l_ref[i, h]] + [jnp.broadcast_to(column(s, 3), (width, HD)) for s in stats]
            numers = [n_ref[i, h]] + [p[u * width : (u + 1) * width, :].astype(jnp.float32) for p in packed]
            top = functools.reduce(jnp.maximum, peaks)
            total = jnp.zeros((width, HD), jnp.float32)
            numer = jnp.zeros((width, HD), jnp.float32)
            for m, l, n in zip(peaks, totals, numers):
                f = jnp.exp(m - top)
                total = total + l * f
                numer = numer + n * f
            results[i, h] = numer / total
    for h in range(kh):
        for g in range(group):
            rows = [results[i, h][g * guess : (g + 1) * guess] for i in range(per)]
            at = (h * group + g) * HD
            out_ref[:, at : at + HD] = jnp.concatenate(rows, axis=0).astype(jnp.bfloat16)


def merge(own, packed, group):
    per, kh, width, _ = own[0].shape
    whole = pl.BlockSpec(own[0].shape, lambda n: (0, 0, 0, 0))
    sent = pl.BlockSpec(packed[0].shape, lambda n: (0, 0))
    shape = (per * width // group, kh * group * HD)
    return pl.pallas_call(
        functools.partial(merge_kernel, group),
        grid=(1,),
        out_shape=jax.ShapeDtypeStruct(shape, jnp.bfloat16),
        in_specs=[whole] * 3 + [sent] * len(packed),
        out_specs=pl.BlockSpec(shape, lambda n: (0, 0)),
        compiler_params=pltpu.CompilerParams(vmem_limit_bytes=16 << 20),
        name="merge",
    )(*own, *packed)


def output_kernel(roll, meta, *refs):
    parts = (refs[:roll], refs[roll : 2 * roll])
    w_ref, keep_ref, send_ref, lhs, acc = refs[2 * roll :]
    step = pl.program_id(0)
    steps = pl.num_programs(0)
    zone, tp = meta[0], meta[2]
    block = parts[0][0].shape[0]
    depth = w_ref.shape[0]
    half = step // (steps // 2)

    @pl.when(step == 0)
    def _():
        for h in range(2):
            for k in range(roll):
                at = pl.multiple_of((zone ^ k) * block, block)
                lhs[h, pl.ds(at, block), :] = parts[h][k][...]

    at = pl.multiple_of((step % (steps // 2)) * depth, depth)
    part = jnp.dot(lhs[half, :, pl.ds(at, depth)], w_ref[...], preferred_element_type=jnp.float32)

    @pl.when(step == 0)
    def _():
        acc[...] = part

    @pl.when(step > 0)
    def _():
        acc[...] += part

    @pl.when(step == steps - 1)
    def _():
        rows = keep_ref.shape[0]
        keep_ref[...] = acc[pl.ds(pl.multiple_of(tp * rows, rows), rows), :]
        send_ref[...] = acc[pl.ds(pl.multiple_of((1 - tp) * rows, rows), rows), :].astype(send_ref.dtype)


def output(meta, mine, theirs, w_out):
    roll = len(mine)
    block, cols = mine[0].shape
    depth = 512 if cols % 512 == 0 else cols
    each = cols // depth
    width = w_out.shape[1]
    rows = roll * block
    part = pl.BlockSpec((block, cols), lambda n, meta: (0, 0))

    def weight(n, meta):
        side = jnp.where(n < each, meta[1], 1 - meta[1])
        return (side * each + n % each, 0)

    out = pl.BlockSpec((rows // 2, width), lambda n, meta: (0, 0))
    return pl.pallas_call(
        functools.partial(output_kernel, roll),
        grid_spec=pltpu.PrefetchScalarGridSpec(
            num_scalar_prefetch=1,
            grid=(2 * each,),
            in_specs=[part] * (2 * roll) + [pl.BlockSpec((depth, width), weight)],
            out_specs=(out, out),
            scratch_shapes=[pltpu.VMEM((2, rows, cols), jnp.bfloat16), pltpu.VMEM((rows, width), jnp.float32)],
        ),
        out_shape=(
            jax.ShapeDtypeStruct((rows // 2, width), jnp.float32),
            jax.ShapeDtypeStruct((rows // 2, width), jnp.bfloat16),
        ),
        compiler_params=pltpu.CompilerParams(vmem_limit_bytes=VMEM_ALL),
        cost_estimate=pl.CostEstimate(
            flops=4 * rows * cols * width, bytes_accessed=4 * cols * width, transcendentals=0
        ),
        name="output",
    )(meta, *mine, *theirs, w_out)


def fast_body(
    hidden,
    w_query,
    w_key,
    w_value,
    b_query,
    b_key,
    b_value,
    w_out,
    prefix_keys,
    prefix_values,
    suffix_keys,
    suffix_values,
    suffix_lengths,
    prompt_of,
):
    roll = lax.axis_size("roll")
    kv_heads = w_key.shape[1] // HD
    group = w_query.shape[1] // w_key.shape[1]
    kh = kv_heads // 2
    per = suffix_keys.shape[0]
    block = hidden.shape[0] // roll
    guess = block // per
    scale = 1.0 / math.sqrt(HD)
    zone = lax.axis_index("roll").astype(jnp.int32)
    seq = lax.axis_index("seq").astype(jnp.int32)
    tp = lax.axis_index("tp").astype(jnp.int32)
    meta = jnp.stack([zone, seq, tp])

    def across(x):
        return lax.ppermute(x, "seq", [(0, 1), (1, 0)])

    def hop(x, k):
        return lax.ppermute(x, "roll", [(n, n ^ k) for n in range(roll)])

    send = project(meta, hidden, w_query, w_key, w_value, roll, kh, True)
    got = across(send)
    keep = project(meta, hidden, w_query, w_key, w_value, roll, kh, False)
    terms = tuple(keep[k] + got[k] for k in range(1, roll))
    terms, caches, small = lax.optimization_barrier(
        (terms, (suffix_keys, suffix_values, prefix_keys, prefix_values), (suffix_lengths, b_query, b_key, b_value))
    )
    sums = [hop(term, k + 1) for k, term in enumerate(terms)]

    def other_half(x):
        return across(lax.dynamic_slice_in_dim(x, (1 - seq) * (kh * HD), kh * HD, x.ndim - 1))

    sk_got, sv_got, pk_got, pv_got = [other_half(x) for x in caches]

    row_ids = jnp.arange(hidden.shape[0], dtype=jnp.int32)
    prefix_total = prefix_keys.shape[1] * roll * 2
    positions = (prefix_total + lookup(small[0], row_ids // guess) + row_ids % guess).astype(jnp.float32)
    half = HD // 2
    steps = jnp.arange(half).astype(jnp.float32) * (2.0 / HD)
    freqs = jnp.exp(-math.log(ROPE_BASE) * steps)
    angles = positions[:, None] * freqs[None, :]
    cosine = jnp.cos(angles)
    sine = jnp.sin(angles)
    cosine = jnp.concatenate([cosine, cosine], axis=-1)
    sine = jnp.concatenate([-sine, sine], axis=-1)
    biases = [b[None, :] for b in small[1:]]

    q, k_new, v_new = finish(meta, keep, got, sums, biases, cosine, sine, per)
    queries = [q] + [hop(q, k) for k in range(1, roll)]
    own = own_attention(
        meta, suffix_lengths, q, k_new, v_new, suffix_keys, sk_got, suffix_values, sv_got, scale, guess
    )
    own, packed = prefix_attention(
        meta, prompt_of, queries, prefix_keys, pk_got, prefix_values, pv_got, own, scale
    )
    packed = [hop(p, k + 1) for k, p in enumerate(packed)]
    share = merge(own, packed, group)
    mine = [share] + [hop(share, k) for k in range(1, roll)]
    theirs = [across(m) for m in mine]
    kept, sent = output(meta, mine, theirs, w_out)
    arrived = lax.ppermute(sent, "tp", [(0, 1), (1, 0)])
    return (kept + arrived.astype(jnp.float32)).astype(jnp.bfloat16)


def body(*arrays):
    hidden, w_key, prompt_of, suffix_keys = arrays[0], arrays[2], arrays[13], arrays[10]
    roll = lax.axis_size("roll")
    block = hidden.shape[0] // roll
    fits = (
        lax.axis_size("seq") == 2
        and lax.axis_size("tp") == 2
        and roll & (roll - 1) == 0
        and (w_key.shape[1] // HD) % 2 == 0
        and block % 16 == 0
        and block == suffix_keys.shape[0] * GUESS
        and 6 * suffix_keys.shape[0] * (w_key.shape[1] // HD) <= 2 * HD
        and prompt_of.shape[0] % arrays[8].shape[0] == 0
    )
    return fast_body(*arrays) if fits else general_body(*arrays)


def solution(mesh):
    return jax.shard_map(
        body,
        mesh=mesh,
        in_specs=(
            P("groups", ("roll", "seq")),
            P(("roll", "seq"), "tp"),
            P(("roll", "seq"), "tp"),
            P(("roll", "seq"), "tp"),
            P("tp"),
            P("tp"),
            P("tp"),
            P("tp", ("roll", "seq")),
            P("groups", ("roll", "seq"), "tp"),
            P("groups", ("roll", "seq"), "tp"),
            P(("groups", "roll"), "seq", "tp"),
            P(("groups", "roll"), "seq", "tp"),
            P("groups"),
            P("groups"),
        ),
        out_specs=P(("groups", "tp"), ("roll", "seq")),
        check_vma=False,
    )
```

```python
import functools
import math

import jax
import jax.numpy as jnp
from jax import lax
from jax.experimental import pallas as pl
from jax.experimental.pallas import tpu as pltpu
from jax.sharding import PartitionSpec as P


HD = 128
GUESS = 8


ROPE_BASE = 1000000.0
NEG_FILL = -1e30


def rotate(values, positions):
    half = values.shape[-1] // 2
    steps = jnp.arange(half).astype(jnp.float32) * (2.0 / values.shape[-1])
    freqs = jnp.exp(-math.log(ROPE_BASE) * steps)
    angles = positions[:, None] * freqs[None, :]
    cosine = jnp.cos(angles)[:, None, :]
    sine = jnp.sin(angles)[:, None, :]
    first = values[..., :half]
    second = values[..., half:]
    return jnp.concatenate(
        [first * cosine - second * sine, second * cosine + first * sine], axis=-1
    )


def lookup(table, indices):
    hits = indices[:, None] == jnp.arange(table.shape[0], dtype=jnp.int32)[None, :]
    return jnp.sum(jnp.where(hits, table[None, :], 0), axis=1)


def combine(first, second):
    peak_a, total_a, numer_a = first
    peak_b, total_b, numer_b = second
    peak = jnp.maximum(peak_a, peak_b)
    factor_a = jnp.exp(peak_a - peak)
    factor_b = jnp.exp(peak_b - peak)
    return (
        peak,
        total_a * factor_a + total_b * factor_b,
        numer_a * factor_a[..., None] + numer_b * factor_b[..., None],
    )


def masked_stats(scores, visible, values):
    peak = jnp.max(jnp.where(visible, scores, NEG_FILL), axis=-1)
    weights = jnp.exp(jnp.where(visible, scores - peak[..., None], NEG_FILL))
    total = jnp.sum(weights, axis=-1)
    numer = jnp.einsum(
        "rtkgs,rskd->rtkgd",
        weights.astype(jnp.bfloat16),
        values,
        preferred_element_type=jnp.float32,
    )
    return (peak, total, numer)


def general_body(
    hidden,
    w_query,
    w_key,
    w_value,
    b_query,
    b_key,
    b_value,
    w_out,
    prefix_keys,
    prefix_values,
    suffix_keys,
    suffix_values,
    suffix_lengths,
    prompt_of,
):
    row_count = hidden.shape[0]
    q_heads = w_query.shape[1] // HD
    kv_heads = w_key.shape[1] // HD
    group = q_heads // kv_heads
    prompts = prefix_keys.shape[0]
    pre_dev = prefix_keys.shape[1]
    prefix_total = pre_dev * lax.axis_size(("roll", "seq"))
    per_device = suffix_keys.shape[0]
    suf_dev = suffix_keys.shape[1]
    scale = 1.0 / math.sqrt(HD)
    q_part = jnp.dot(hidden, w_query, preferred_element_type=jnp.float32)
    k_part = jnp.dot(hidden, w_key, preferred_element_type=jnp.float32)
    v_part = jnp.dot(hidden, w_value, preferred_element_type=jnp.float32)
    q_sum, k_sum, v_sum = lax.psum((q_part, k_part, v_part), ("roll", "seq"))
    count = q_sum.shape[0]
    row_ids = jnp.arange(count, dtype=jnp.int32)
    owner_ids = row_ids // GUESS
    positions = (prefix_total + lookup(suffix_lengths, owner_ids) + row_ids % GUESS).astype(
        jnp.float32
    )
    q_rot = rotate((q_sum + b_query.astype(jnp.float32)).reshape(count, q_heads, HD), positions)
    k_rot = rotate((k_sum + b_key.astype(jnp.float32)).reshape(count, kv_heads, HD), positions)
    v_fin = (v_sum + b_value.astype(jnp.float32)).reshape(count, kv_heads, HD)
    query = q_rot.astype(jnp.bfloat16)
    key_new = k_rot.astype(jnp.bfloat16)
    value_new = v_fin.astype(jnp.bfloat16)
    query_grid = query.reshape(row_count, kv_heads, group, HD)
    owners_all = jnp.arange(row_count, dtype=jnp.int32) // GUESS
    row_prompt = lookup(prompt_of, owners_all)
    pre_keys = prefix_keys.reshape(prompts, pre_dev, kv_heads, HD)
    pre_values = prefix_values.reshape(prompts, pre_dev, kv_heads, HD)
    peak_all = jnp.full((row_count, kv_heads, group), NEG_FILL, jnp.float32)
    total_all = jnp.zeros((row_count, kv_heads, group), jnp.float32)
    numer_all = jnp.zeros((row_count, kv_heads, group, HD), jnp.float32)
    for prompt in range(prompts):
        scores = (
            jnp.einsum(
                "tkgd,skd->tkgs", query_grid, pre_keys[prompt], preferred_element_type=jnp.float32
            )
            * scale
        )
        block_peak = jnp.max(scores, axis=-1)
        weights = jnp.exp(scores - block_peak[..., None])
        block_numer = jnp.einsum(
            "tkgs,skd->tkgd",
            weights.astype(jnp.bfloat16),
            pre_values[prompt],
            preferred_element_type=jnp.float32,
        )
        picked = (row_prompt == prompt)[:, None, None]
        peak_all = jnp.where(picked, block_peak, peak_all)
        total_all = jnp.where(picked, jnp.sum(weights, axis=-1), total_all)
        numer_all = jnp.where(picked[..., None], block_numer, numer_all)
    first_rollout = lax.axis_index("roll") * per_device
    seq_index = lax.axis_index("seq")
    local_len = lax.dynamic_slice_in_dim(suffix_lengths, first_rollout, per_device, 0)
    live = jnp.clip(local_len - seq_index * suf_dev, 0, suf_dev)
    row_start = first_rollout * GUESS
    local_rows = per_device * GUESS
    query_local = lax.dynamic_slice_in_dim(query_grid, row_start, local_rows, 0).reshape(
        per_device, GUESS, kv_heads, group, HD
    )
    suf_keys = suffix_keys.reshape(per_device, suf_dev, kv_heads, HD)
    suf_values = suffix_values.reshape(per_device, suf_dev, kv_heads, HD)
    scores = (
        jnp.einsum("rtkgd,rskd->rtkgs", query_local, suf_keys, preferred_element_type=jnp.float32)
        * scale
    )
    visible = (jnp.arange(suf_dev, dtype=jnp.int32)[None, :] < live[:, None])[
        :, None, None, None, :
    ]
    suffix_part = masked_stats(scores, visible, suf_values)
    key_local = lax.dynamic_slice_in_dim(key_new, row_start, local_rows, 0).reshape(
        per_device, GUESS, kv_heads, HD
    )
    value_local = lax.dynamic_slice_in_dim(value_new, row_start, local_rows, 0).reshape(
        per_device, GUESS, kv_heads, HD
    )
    new_scores = (
        jnp.einsum("rtkgd,rskd->rtkgs", query_local, key_local, preferred_element_type=jnp.float32)
        * scale
    )
    guess_ids = jnp.arange(GUESS, dtype=jnp.int32)
    causal = (guess_ids[None, :] <= guess_ids[:, None]) & (seq_index == 0)
    guess_part = masked_stats(new_scores, causal[None, :, None, None, :], value_local)
    prefix_local = (
        lax.dynamic_slice_in_dim(peak_all, row_start, local_rows, 0).reshape(
            per_device, GUESS, kv_heads, group
        ),
        lax.dynamic_slice_in_dim(total_all, row_start, local_rows, 0).reshape(
            per_device, GUESS, kv_heads, group
        ),
        lax.dynamic_slice_in_dim(numer_all, row_start, local_rows, 0).reshape(
            per_device, GUESS, kv_heads, group, HD
        ),
    )
    peak_loc, total_loc, numer_loc = combine(combine(prefix_local, suffix_part), guess_part)
    peak_all = lax.dynamic_update_slice_in_dim(
        peak_all, peak_loc.reshape(local_rows, kv_heads, group), row_start, 0
    )
    total_all = lax.dynamic_update_slice_in_dim(
        total_all, total_loc.reshape(local_rows, kv_heads, group), row_start, 0
    )
    numer_all = lax.dynamic_update_slice_in_dim(
        numer_all, numer_loc.reshape(local_rows, kv_heads, group, HD), row_start, 0
    )
    peaks, totals, numers = (
        lax.all_to_all(peak_all[None], ("roll", "seq"), split_axis=1, concat_axis=0, tiled=True),
        lax.all_to_all(total_all[None], ("roll", "seq"), split_axis=1, concat_axis=0, tiled=True),
        lax.all_to_all(numer_all[None], ("roll", "seq"), split_axis=1, concat_axis=0, tiled=True),
    )
    peak_top = jnp.max(peaks, axis=0)
    factors = jnp.exp(peaks - peak_top[None])
    share = (
        jnp.sum(numers * factors[..., None], axis=0) / jnp.sum(totals * factors, axis=0)[..., None]
    )
    share = share.astype(jnp.bfloat16).reshape(share.shape[0], q_heads * HD)
    attention = lax.all_gather(share, ("roll", "seq"), axis=0, tiled=True)
    summed = lax.psum_scatter(
        jnp.dot(attention, w_out, preferred_element_type=jnp.float32),
        "tp",
        scatter_dimension=0,
        tiled=True,
    )
    return summed.astype(jnp.bfloat16)


VMEM_MOST = 66900000


def contract_last(a, b):
    return lax.dot_general(a, b, (((1,), (1,)), ((), ())), preferred_element_type=jnp.float32)


def project_kernel(flip, x_ref, wq_ref, wk_ref, wv_ref, out_ref, x_all, wq, wk, wv, sems):
    zone = lax.axis_index("roll")
    seq = lax.axis_index("seq")
    half = 1 - seq if flip else seq
    roll, kh, block, width = out_ref.shape
    wide = width - 2 * HD
    chunks = wq.shape[0]
    span = wq.shape[2]

    fetch = pltpu.make_async_copy(x_ref, x_all, sems.at[chunks + 2])
    fetch.start()
    copies = []
    for c in range(chunks):
        at = pl.multiple_of(half * (kh * wide) + c * span, span)
        copies.append(pltpu.make_async_copy(wq_ref.at[:, pl.ds(at, span)], wq.at[c], sems.at[c]))
    at = pl.multiple_of(half * (kh * HD), kh * HD)
    copies.append(pltpu.make_async_copy(wk_ref.at[:, pl.ds(at, kh * HD)], wk, sems.at[chunks]))
    copies.append(pltpu.make_async_copy(wv_ref.at[:, pl.ds(at, kh * HD)], wv, sems.at[chunks + 1]))
    for copy in copies:
        copy.start()
    fetch.wait()
    x = x_all[...]

    def place(part, j, at):
        for b in range(roll):
            out_ref[b ^ zone, j, :, at : at + part.shape[1]] = part[b * block : (b + 1) * block]

    for c in range(chunks):
        copies[c].wait()
        part = jnp.dot(x, wq[c], preferred_element_type=jnp.float32)
        place(part, c * span // wide, c * span % wide)
    for copy, w, at in ((copies[chunks], wk, wide), (copies[chunks + 1], wv, wide + HD)):
        copy.wait()
        part = jnp.dot(x, w[...], preferred_element_type=jnp.float32)
        for j in range(kh):
            place(part[:, j * HD : (j + 1) * HD], j, at)


def project(hidden, w_query, w_key, w_value, roll, kh, flip):
    rows, depth = hidden.shape
    kv_heads = w_key.shape[1] // HD
    wide = w_query.shape[1] // kv_heads
    block = rows // roll
    width = wide + 2 * HD
    span = min(wide, 512)
    chunks = kh * wide // span
    hbm = pl.BlockSpec(memory_space=pltpu.HBM)
    vmem = pl.BlockSpec(memory_space=pltpu.VMEM)
    return pl.pallas_call(
        functools.partial(project_kernel, flip),
        out_shape=jax.ShapeDtypeStruct((roll, kh, block, width), jnp.float32),
        in_specs=[hbm] * 4,
        out_specs=vmem,
        scratch_shapes=[
            pltpu.VMEM((rows, depth), jnp.bfloat16),
            pltpu.VMEM((chunks, depth, span), jnp.bfloat16),
            pltpu.VMEM((depth, kh * HD), jnp.bfloat16),
            pltpu.VMEM((depth, kh * HD), jnp.bfloat16),
            pltpu.SemaphoreType.DMA((chunks + 3,)),
        ],
        compiler_params=pltpu.CompilerParams(vmem_limit_bytes=VMEM_MOST - 4 * rows * width * kh),
        cost_estimate=pl.CostEstimate(
            flops=2 * rows * depth * width * kh,
            bytes_accessed=2 * depth * width * kh + 4 * rows * width * kh,
            transcendentals=0,
        ),
        name="project_send" if flip else "project_keep",
    )(hidden, w_query, w_key, w_value)


def finish_kernel(group, per, meta, keep_ref, got_ref, *refs):
    others = refs[:-8]
    bq_ref, bk_ref, bv_ref, cos_ref, sin_ref, q_ref, k_ref, v_ref = refs[-8:]
    kh = keep_ref.shape[1]
    guess = cos_ref.shape[0] // per
    cosine = cos_ref[...]
    sine = sin_ref[...]

    def total(j, g):
        at = slice(g * HD, (g + 1) * HD)
        u = keep_ref[0, j, :, at] + got_ref[0, j, :, at]
        for o in others:
            u = u + o[j, :, at]
        if g < group:
            bias = bq_ref[:, (j * group + g) * HD : (j * group + g + 1) * HD]
        else:
            bias = (bk_ref if g == group else bv_ref)[:, j * HD : (j + 1) * HD]
        return u + bias.astype(jnp.float32)

    def turn(u):
        return u * cosine + pltpu.roll(u, HD // 2, 1) * sine

    for j in range(kh):
        for g in range(0, group, 2):
            one = turn(total(j, g))
            two = turn(total(j, g + 1))
            for i in range(per):
                span = slice(i * guess, (i + 1) * guess)
                both = jnp.concatenate([one[span], two[span]], axis=0)
                q_ref[i, j, g * guess : (g + 2) * guess, :] = both.astype(jnp.bfloat16)
        k_ref[j] = turn(total(j, group)).astype(jnp.bfloat16)
        v_ref[j] = total(j, group + 1).astype(jnp.bfloat16)


def finish(meta, keep, got, others, biases, cosine, sine, per):
    _, kh, block, width = keep.shape
    group = width // HD - 2
    guess = block // per
    first = pl.BlockSpec((1, kh, block, width), lambda n, meta: (0, 0, 0, 0))
    part = pl.BlockSpec((kh, block, width), lambda n, meta: (0, 0, 0))
    table = pl.BlockSpec((block, HD), lambda n, meta: (meta[0], 0))

    def half(bias):
        return pl.BlockSpec((1, bias.shape[1] // 2), lambda n, meta: (0, meta[1]))

    return pl.pallas_call(
        functools.partial(finish_kernel, group, per),
        grid_spec=pltpu.PrefetchScalarGridSpec(
            num_scalar_prefetch=1,
            grid=(1,),
            in_specs=[first, first] + [part] * len(others) + [half(b) for b in biases] + [table, table],
            out_specs=(
                pl.BlockSpec((per, kh, group * guess, HD), lambda n, meta: (0, 0, 0, 0)),
                pl.BlockSpec((kh, block, HD), lambda n, meta: (0, 0, 0)),
                pl.BlockSpec((kh, block, HD), lambda n, meta: (0, 0, 0)),
            ),
        ),
        out_shape=(
            jax.ShapeDtypeStruct((per, kh, group * guess, HD), jnp.bfloat16),
            jax.ShapeDtypeStruct((kh, block, HD), jnp.bfloat16),
            jax.ShapeDtypeStruct((kh, block, HD), jnp.bfloat16),
        ),
        compiler_params=pltpu.CompilerParams(vmem_limit_bytes=16 << 20),
        name="finish",
    )(meta, keep, got, *others, *biases, cosine, sine)


def own_kernel(scale, guess, meta, lengths, q_ref, kn_ref, vn_ref, k0_ref, k1_ref, v0_ref, v1_ref, n_ref, m_ref, l_ref):
    per, kh, width, _ = q_ref.shape
    span = k0_ref.shape[1]
    seq = meta[1]
    fresh = kn_ref.shape[1]
    key_id = lax.broadcasted_iota(jnp.int32, (width, span), 1)
    new_id = lax.broadcasted_iota(jnp.int32, (width, fresh), 1)
    row_id = lax.broadcasted_iota(jnp.int32, (width, fresh), 0) % guess
    for i in range(per):
        length = lengths[meta[0] * per + i]
        sees = (key_id < length - seq * span, key_id < length - (1 - seq) * span)
        causal = (new_id >= i * guess) & (new_id - i * guess <= row_id)
        sees = sees + (causal,)
        for j in range(kh):
            q = q_ref[i, j]
            at = slice(j * HD, (j + 1) * HD)
            keys = (k0_ref[i, :, at], k1_ref[i, :, at], kn_ref[j])
            values = (v0_ref[i, :, at], v1_ref[i, :, at], vn_ref[j])
            scores = [jnp.where(see, contract_last(q, k) * scale, NEG_FILL) for k, see in zip(keys, sees)]
            peak = jnp.max(scores[0], axis=1, keepdims=True)
            for s in scores[1:]:
                peak = jnp.maximum(peak, jnp.max(s, axis=1, keepdims=True))
            total = jnp.zeros((width, 1), jnp.float32)
            numer = jnp.zeros((width, HD), jnp.float32)
            for s, v in zip(scores, values):
                w = jnp.exp(s - peak)
                total = total + jnp.sum(w, axis=1, keepdims=True)
                numer = numer + jnp.dot(w.astype(jnp.bfloat16), v, preferred_element_type=jnp.float32)
            n_ref[i, j] = numer
            m_ref[i, j] = jnp.broadcast_to(peak, (width, HD))
            l_ref[i, j] = jnp.broadcast_to(total, (width, HD))


def own_attention(meta, lengths, q, k_new, v_new, keys, keys_got, values, values_got, scale, guess):
    per, kh, width, _ = q.shape
    span = keys.shape[1]
    cols = kh * HD
    local = pl.BlockSpec((per, span, cols), lambda n, meta, lengths: (0, 0, meta[1]))
    got = pl.BlockSpec((per, span, cols), lambda n, meta, lengths: (0, 0, 0))
    fresh = pl.BlockSpec(k_new.shape, lambda n, meta, lengths: (0, 0, 0))
    whole = pl.BlockSpec(q.shape, lambda n, meta, lengths: (0, 0, 0, 0))
    out = jax.ShapeDtypeStruct(q.shape, jnp.float32)
    elements = per * kh * width * span * 2
    return pl.pallas_call(
        functools.partial(own_kernel, scale, guess),
        grid_spec=pltpu.PrefetchScalarGridSpec(
            num_scalar_prefetch=2,
            grid=(1,),
            in_specs=[whole, fresh, fresh, local, got, local, got],
            out_specs=(whole, whole, whole),
        ),
        out_shape=(out, out, out),
        compiler_params=pltpu.CompilerParams(vmem_limit_bytes=24 << 20),
        cost_estimate=pl.CostEstimate(
            flops=4 * elements * HD, bytes_accessed=8 * per * span * cols, transcendentals=elements
        ),
        name="own_attention",
    )(meta, lengths, q, k_new, v_new, keys, keys_got, values, values_got)


def split_three(x):
    high = x.astype(jnp.bfloat16).astype(jnp.float32)
    rest = x - high
    middle = rest.astype(jnp.bfloat16).astype(jnp.float32)
    return high, middle, rest - middle


def prefix_kernel(scale, roll, meta, prompts, *refs):
    q_refs = refs[:roll]
    k0_ref, k1_ref, v0_ref, v1_ref, on_ref, om_ref, ol_ref = refs[roll : roll + 7]
    n_out, m_out, l_out = refs[roll + 7 : roll + 10]
    packed = refs[roll + 10 : 2 * roll + 9]
    q_all, n_all, m_all, l_all, order = refs[2 * roll + 9 :]
    per, kh, width, _ = q_refs[0].shape
    prompt = pl.program_id(0)
    j = pl.program_id(1)
    share = roll * per // pl.num_programs(0)

    @pl.when((prompt == 0) & (j == 0))
    def _():
        for k in range(roll):
            q_all[k * per : (k + 1) * per] = q_refs[k][...]

    @pl.when(j == 0)
    def _():
        filled = jnp.int32(0)
        for k in range(roll):
            for i in range(per):
                chosen = prompts[(meta[0] ^ k) * per + i] == prompt

                @pl.when(chosen)
                def _():
                    order[filled] = k * per + i

                filled = filled + chosen.astype(jnp.int32)

    ids = [order[n] for n in range(share)]
    q = jnp.concatenate([q_all[at, j] for at in ids], axis=0)
    scores = [contract_last(q, k_ref[0]) * scale for k_ref in (k0_ref, k1_ref)]
    peak = jnp.maximum(
        jnp.max(scores[0], axis=1, keepdims=True), jnp.max(scores[1], axis=1, keepdims=True)
    )
    total = jnp.zeros(peak.shape, jnp.float32)
    numer = jnp.zeros((share * width, HD), jnp.float32)
    for s, v_ref in zip(scores, (v0_ref, v1_ref)):
        w = jnp.exp(s - peak)
        total = total + jnp.sum(w, axis=1, keepdims=True)
        numer = numer + jnp.dot(w.astype(jnp.bfloat16), v_ref[0], preferred_element_type=jnp.float32)
    peak = jnp.broadcast_to(peak, numer.shape)
    total = jnp.broadcast_to(total, numer.shape)
    for n, at in enumerate(ids):
        span = slice(n * width, (n + 1) * width)
        n_all[at, j] = numer[span]
        m_all[at, j] = peak[span]
        l_all[at, j] = total[span]

    @pl.when((prompt == pl.num_programs(0) - 1) & (j == kh - 1))
    def _():
        for i in range(per):
            for h in range(kh):
                m_a, m_b = m_all[i, h], om_ref[i, h]
                peak = jnp.maximum(m_a, m_b)
                f_a, f_b = jnp.exp(m_a - peak), jnp.exp(m_b - peak)
                m_out[i, h] = peak
                l_out[i, h] = l_all[i, h] * f_a + ol_ref[i, h] * f_b
                n_out[i, h] = n_all[i, h] * f_a + on_ref[i, h] * f_b
        lane = lax.broadcasted_iota(jnp.int32, (width, HD), 1)
        for k in range(1, roll):
            stats = jnp.zeros((width, HD), jnp.float32)
            for i in range(per):
                for h in range(kh):
                    u = i * kh + h
                    packed[k - 1][u * width : (u + 1) * width, :] = n_all[k * per + i, h].astype(jnp.bfloat16)
                    pieces = split_three(m_all[k * per + i, h]) + split_three(l_all[k * per + i, h])
                    for c, piece in enumerate(pieces):
                        stats = jnp.where(lane == 6 * u + c, piece, stats)
            u = per * kh
            packed[k - 1][u * width : (u + 1) * width, :] = stats.astype(jnp.bfloat16)


def prefix_attention(meta, prompt_of, queries, keys, keys_got, values, values_got, own, scale):
    roll = len(queries)
    per, kh, width, _ = queries[0].shape
    prompts, span, _ = keys.shape
    local = pl.BlockSpec((1, span, HD), lambda p, j, meta, prompts: (p, 0, meta[1] * kh + j))
    got = pl.BlockSpec((1, span, HD), lambda p, j, meta, prompts: (p, 0, j))
    whole = pl.BlockSpec(queries[0].shape, lambda p, j, meta, prompts: (0, 0, 0, 0))
    rows = (per * kh + 1) * width
    sent = pl.BlockSpec((rows, HD), lambda p, j, meta, prompts: (0, 0))
    out = jax.ShapeDtypeStruct(queries[0].shape, jnp.float32)
    elements = roll * per * kh * width * span * 2
    everything = (roll * per, kh, width, HD)
    outs = pl.pallas_call(
        functools.partial(prefix_kernel, scale, roll),
        grid_spec=pltpu.PrefetchScalarGridSpec(
            num_scalar_prefetch=2,
            grid=(prompts, kh),
            in_specs=[whole] * roll + [local, got, local, got] + [whole] * 3,
            out_specs=[whole] * 3 + [sent] * (roll - 1),
            scratch_shapes=[pltpu.VMEM(everything, jnp.bfloat16)] + [pltpu.VMEM(everything, jnp.float32)] * 3
            + [pltpu.SMEM((roll * per,), jnp.int32)],
        ),
        out_shape=[out] * 3 + [jax.ShapeDtypeStruct((rows, HD), jnp.bfloat16)] * (roll - 1),
        compiler_params=pltpu.CompilerParams(vmem_limit_bytes=24 << 20),
        cost_estimate=pl.CostEstimate(
            flops=4 * elements * HD, bytes_accessed=8 * prompts * span * kh * HD, transcendentals=elements
        ),
        name="prefix_attention",
    )(meta, prompt_of, *queries, keys, keys_got, values, values_got, *own)
    return outs[:3], outs[3:]


def merge_kernel(group, n_ref, m_ref, l_ref, *refs):
    packed, out_ref = refs[:-1], refs[-1]
    per, kh, width, _ = n_ref.shape
    guess = width // group
    stats = [p[per * kh * width :, :].astype(jnp.float32) for p in packed]
    results = {}
    for i in range(per):
        for h in range(kh):
            u = i * kh + h

            def column(s, c):
                c = 6 * u + c
                return s[:, c : c + 1] + s[:, c + 1 : c + 2] + s[:, c + 2 : c + 3]

            peaks = [m_ref[i, h]] + [jnp.broadcast_to(column(s, 0), (width, HD)) for s in stats]
            totals = [l_ref[i, h]] + [jnp.broadcast_to(column(s, 3), (width, HD)) for s in stats]
            numers = [n_ref[i, h]] + [p[u * width : (u + 1) * width, :].astype(jnp.float32) for p in packed]
            top = functools.reduce(jnp.maximum, peaks)
            total = jnp.zeros((width, HD), jnp.float32)
            numer = jnp.zeros((width, HD), jnp.float32)
            for m, l, n in zip(peaks, totals, numers):
                f = jnp.exp(m - top)
                total = total + l * f
                numer = numer + n * f
            results[i, h] = numer / total
    for h in range(kh):
        for g in range(group):
            rows = [results[i, h][g * guess : (g + 1) * guess] for i in range(per)]
            at = (h * group + g) * HD
            out_ref[:, at : at + HD] = jnp.concatenate(rows, axis=0).astype(jnp.bfloat16)


def merge(own, packed, group):
    per, kh, width, _ = own[0].shape
    whole = pl.BlockSpec(own[0].shape, lambda n: (0, 0, 0, 0))
    sent = pl.BlockSpec(packed[0].shape, lambda n: (0, 0))
    shape = (per * width // group, kh * group * HD)
    return pl.pallas_call(
        functools.partial(merge_kernel, group),
        grid=(1,),
        out_shape=jax.ShapeDtypeStruct(shape, jnp.bfloat16),
        in_specs=[whole] * 3 + [sent] * len(packed),
        out_specs=pl.BlockSpec(shape, lambda n: (0, 0)),
        compiler_params=pltpu.CompilerParams(vmem_limit_bytes=16 << 20),
        name="merge",
    )(*own, *packed)


def output_kernel(roll, *refs):
    parts = (refs[:roll], refs[roll : 2 * roll])
    w_ref, keep_ref, send_ref, w, lhs, sems = refs[2 * roll :]
    zone, seq, tp = lax.axis_index("roll"), lax.axis_index("seq"), lax.axis_index("tp")
    block, cols = parts[0][0].shape
    chunks, depth, _ = w.shape
    each = chunks // 2
    copies = []
    for c in range(chunks):
        side = seq if c < each else 1 - seq
        at = pl.multiple_of(side * cols + (c % each) * depth, depth)
        copies.append(pltpu.make_async_copy(w_ref.at[pl.ds(at, depth), :], w.at[c], sems.at[c]))
    for copy in copies:
        copy.start()
    for h in range(2):
        for k in range(roll):
            at = pl.multiple_of((zone ^ k ^ (tp * (roll // 2))) * block, block)
            lhs[h, pl.ds(at, block), :] = parts[h][k][...]
    total = None
    for c in range(chunks):
        copies[c].wait()
        at = (c % each) * depth
        part = jnp.dot(lhs[c // each, :, at : at + depth], w[c], preferred_element_type=jnp.float32)
        total = part if c == 0 else total + part
    rows = keep_ref.shape[0]
    keep_ref[...] = total[:rows]
    send_ref[...] = total[rows:].astype(send_ref.dtype)


def output(mine, theirs, w_out):
    roll = len(mine)
    block, cols = mine[0].shape
    depth = 512 if cols % 512 == 0 else cols
    chunks = 2 * cols // depth
    width = w_out.shape[1]
    rows = roll * block
    vmem = pl.BlockSpec(memory_space=pltpu.VMEM)
    return pl.pallas_call(
        functools.partial(output_kernel, roll),
        in_specs=[vmem] * (2 * roll) + [pl.BlockSpec(memory_space=pltpu.HBM)],
        out_specs=(vmem, vmem),
        scratch_shapes=[
            pltpu.VMEM((chunks, depth, width), jnp.bfloat16),
            pltpu.VMEM((2, rows, cols), jnp.bfloat16),
            pltpu.SemaphoreType.DMA((chunks,)),
        ],
        out_shape=(
            jax.ShapeDtypeStruct((rows // 2, width), jnp.float32),
            jax.ShapeDtypeStruct((rows // 2, width), jnp.bfloat16),
        ),
        compiler_params=pltpu.CompilerParams(vmem_limit_bytes=24 << 20),
        cost_estimate=pl.CostEstimate(
            flops=4 * rows * cols * width, bytes_accessed=4 * cols * width, transcendentals=0
        ),
        name="output",
    )(*mine, *theirs, w_out)


def fast_body(
    hidden,
    w_query,
    w_key,
    w_value,
    b_query,
    b_key,
    b_value,
    w_out,
    prefix_keys,
    prefix_values,
    suffix_keys,
    suffix_values,
    suffix_lengths,
    prompt_of,
):
    roll = lax.axis_size("roll")
    kv_heads = w_key.shape[1] // HD
    group = w_query.shape[1] // w_key.shape[1]
    kh = kv_heads // 2
    per = suffix_keys.shape[0]
    block = hidden.shape[0] // roll
    guess = block // per
    scale = 1.0 / math.sqrt(HD)
    zone = lax.axis_index("roll").astype(jnp.int32)
    seq = lax.axis_index("seq").astype(jnp.int32)
    tp = lax.axis_index("tp").astype(jnp.int32)

    def across(x):
        return lax.ppermute(x, "seq", [(0, 1), (1, 0)])

    def hop(x, k):
        return lax.ppermute(x, "roll", [(n, n ^ k) for n in range(roll)])

    def hops(pick):
        sent = {k: hop(pick(k), k) for k in reversed(range(1, roll))}
        return [sent[k] for k in range(1, roll)]

    send = project(hidden, w_query, w_key, w_value, roll, kh, True)
    got = across(send)
    keep = project(hidden, w_query, w_key, w_value, roll, kh, False)
    terms = tuple(keep[k] + got[k] for k in range(1, roll))
    caches = (suffix_keys, suffix_values, prefix_keys, prefix_values)
    terms, small = lax.optimization_barrier((terms, (suffix_lengths, b_query, b_key, b_value, zone, seq, *caches)))
    meta = jnp.stack(small[4:6])
    sums = hops(lambda k: terms[k - 1])
    caches = small[6:]

    def other_half(x):
        return across(lax.dynamic_slice_in_dim(x, (1 - seq) * (kh * HD), kh * HD, x.ndim - 1))

    sk_got, sv_got, pk_got, pv_got = [other_half(x) for x in caches]

    row_ids = jnp.arange(hidden.shape[0], dtype=jnp.int32)
    prefix_total = prefix_keys.shape[1] * roll * 2
    positions = (prefix_total + lookup(small[0], row_ids // guess) + row_ids % guess).astype(jnp.float32)
    half = HD // 2
    steps = jnp.arange(half).astype(jnp.float32) * (2.0 / HD)
    freqs = jnp.exp(-math.log(ROPE_BASE) * steps)
    angles = positions[:, None] * freqs[None, :]
    cosine = jnp.cos(angles)
    sine = jnp.sin(angles)
    cosine = jnp.concatenate([cosine, cosine], axis=-1)
    sine = jnp.concatenate([-sine, sine], axis=-1)
    biases = [b[None, :] for b in small[1:4]]

    q, k_new, v_new = finish(meta, keep, got, sums, biases, cosine, sine, per)
    queries = [q] + hops(lambda k: q)
    own = own_attention(
        meta, suffix_lengths, q, k_new, v_new, suffix_keys, sk_got, suffix_values, sv_got, scale, guess
    )
    own, packed = prefix_attention(
        meta, prompt_of, queries, prefix_keys, pk_got, prefix_values, pv_got, own, scale
    )
    packed = hops(lambda k: packed[k - 1])
    share = merge(own, packed, group)
    mine = [share] + hops(lambda k: share)
    theirs = [across(m) for m in mine]
    kept, sent = output(mine, theirs, w_out)
    arrived = lax.ppermute(sent, "tp", [(0, 1), (1, 0)])
    return (kept + arrived.astype(jnp.float32)).astype(jnp.bfloat16)


def body(*arrays):
    hidden, w_key, prompt_of, suffix_keys = arrays[0], arrays[2], arrays[13], arrays[10]
    roll = lax.axis_size("roll")
    block = hidden.shape[0] // roll
    fits = (
        lax.axis_size("seq") == 2
        and lax.axis_size("tp") == 2
        and roll & (roll - 1) == 0
        and (w_key.shape[1] // HD) % 2 == 0
        and block % 16 == 0
        and block == suffix_keys.shape[0] * GUESS
        and 6 * suffix_keys.shape[0] * (w_key.shape[1] // HD) <= 2 * HD
        and prompt_of.shape[0] % arrays[8].shape[0] == 0
    )
    if not fits:
        return general_body(*arrays)
    return fast_body(*arrays)


def solution(mesh):
    return jax.shard_map(
        body,
        mesh=mesh,
        in_specs=(
            P("groups", ("roll", "seq")),
            P(("roll", "seq"), "tp"),
            P(("roll", "seq"), "tp"),
            P(("roll", "seq"), "tp"),
            P("tp"),
            P("tp"),
            P("tp"),
            P("tp", ("roll", "seq")),
            P("groups", ("roll", "seq"), "tp"),
            P("groups", ("roll", "seq"), "tp"),
            P(("groups", "roll"), "seq", "tp"),
            P(("groups", "roll"), "seq", "tp"),
            P("groups"),
            P("groups"),
        ),
        out_specs=P(("groups", "tp"), ("roll", "seq")),
        check_vma=False,
    )
```

```python
import functools
import math

import jax
import jax.numpy as jnp
from jax import lax
from jax.experimental import pallas as pl
from jax.experimental.pallas import tpu as pltpu
from jax.sharding import PartitionSpec as P


HD = 128
GUESS = 8


ROPE_BASE = 1000000.0
NEG_FILL = -1e30


def rotate(values, positions):
    half = values.shape[-1] // 2
    steps = jnp.arange(half).astype(jnp.float32) * (2.0 / values.shape[-1])
    freqs = jnp.exp(-math.log(ROPE_BASE) * steps)
    angles = positions[:, None] * freqs[None, :]
    cosine = jnp.cos(angles)[:, None, :]
    sine = jnp.sin(angles)[:, None, :]
    first = values[..., :half]
    second = values[..., half:]
    return jnp.concatenate(
        [first * cosine - second * sine, second * cosine + first * sine], axis=-1
    )


def lookup(table, indices):
    hits = indices[:, None] == jnp.arange(table.shape[0], dtype=jnp.int32)[None, :]
    return jnp.sum(jnp.where(hits, table[None, :], 0), axis=1)


def combine(first, second):
    peak_a, total_a, numer_a = first
    peak_b, total_b, numer_b = second
    peak = jnp.maximum(peak_a, peak_b)
    factor_a = jnp.exp(peak_a - peak)
    factor_b = jnp.exp(peak_b - peak)
    return (
        peak,
        total_a * factor_a + total_b * factor_b,
        numer_a * factor_a[..., None] + numer_b * factor_b[..., None],
    )


def masked_stats(scores, visible, values):
    peak = jnp.max(jnp.where(visible, scores, NEG_FILL), axis=-1)
    weights = jnp.exp(jnp.where(visible, scores - peak[..., None], NEG_FILL))
    total = jnp.sum(weights, axis=-1)
    numer = jnp.einsum(
        "rtkgs,rskd->rtkgd",
        weights.astype(jnp.bfloat16),
        values,
        preferred_element_type=jnp.float32,
    )
    return (peak, total, numer)


def general_body(
    hidden,
    w_query,
    w_key,
    w_value,
    b_query,
    b_key,
    b_value,
    w_out,
    prefix_keys,
    prefix_values,
    suffix_keys,
    suffix_values,
    suffix_lengths,
    prompt_of,
):
    row_count = hidden.shape[0]
    q_heads = w_query.shape[1] // HD
    kv_heads = w_key.shape[1] // HD
    group = q_heads // kv_heads
    prompts = prefix_keys.shape[0]
    pre_dev = prefix_keys.shape[1]
    prefix_total = pre_dev * lax.axis_size(("roll", "seq"))
    per_device = suffix_keys.shape[0]
    suf_dev = suffix_keys.shape[1]
    scale = 1.0 / math.sqrt(HD)
    q_part = jnp.dot(hidden, w_query, preferred_element_type=jnp.float32)
    k_part = jnp.dot(hidden, w_key, preferred_element_type=jnp.float32)
    v_part = jnp.dot(hidden, w_value, preferred_element_type=jnp.float32)
    q_sum, k_sum, v_sum = lax.psum((q_part, k_part, v_part), ("roll", "seq"))
    count = q_sum.shape[0]
    row_ids = jnp.arange(count, dtype=jnp.int32)
    owner_ids = row_ids // GUESS
    positions = (prefix_total + lookup(suffix_lengths, owner_ids) + row_ids % GUESS).astype(
        jnp.float32
    )
    q_rot = rotate((q_sum + b_query.astype(jnp.float32)).reshape(count, q_heads, HD), positions)
    k_rot = rotate((k_sum + b_key.astype(jnp.float32)).reshape(count, kv_heads, HD), positions)
    v_fin = (v_sum + b_value.astype(jnp.float32)).reshape(count, kv_heads, HD)
    query = q_rot.astype(jnp.bfloat16)
    key_new = k_rot.astype(jnp.bfloat16)
    value_new = v_fin.astype(jnp.bfloat16)
    query_grid = query.reshape(row_count, kv_heads, group, HD)
    owners_all = jnp.arange(row_count, dtype=jnp.int32) // GUESS
    row_prompt = lookup(prompt_of, owners_all)
    pre_keys = prefix_keys.reshape(prompts, pre_dev, kv_heads, HD)
    pre_values = prefix_values.reshape(prompts, pre_dev, kv_heads, HD)
    peak_all = jnp.full((row_count, kv_heads, group), NEG_FILL, jnp.float32)
    total_all = jnp.zeros((row_count, kv_heads, group), jnp.float32)
    numer_all = jnp.zeros((row_count, kv_heads, group, HD), jnp.float32)
    for prompt in range(prompts):
        scores = (
            jnp.einsum(
                "tkgd,skd->tkgs", query_grid, pre_keys[prompt], preferred_element_type=jnp.float32
            )
            * scale
        )
        block_peak = jnp.max(scores, axis=-1)
        weights = jnp.exp(scores - block_peak[..., None])
        block_numer = jnp.einsum(
            "tkgs,skd->tkgd",
            weights.astype(jnp.bfloat16),
            pre_values[prompt],
            preferred_element_type=jnp.float32,
        )
        picked = (row_prompt == prompt)[:, None, None]
        peak_all = jnp.where(picked, block_peak, peak_all)
        total_all = jnp.where(picked, jnp.sum(weights, axis=-1), total_all)
        numer_all = jnp.where(picked[..., None], block_numer, numer_all)
    first_rollout = lax.axis_index("roll") * per_device
    seq_index = lax.axis_index("seq")
    local_len = lax.dynamic_slice_in_dim(suffix_lengths, first_rollout, per_device, 0)
    live = jnp.clip(local_len - seq_index * suf_dev, 0, suf_dev)
    row_start = first_rollout * GUESS
    local_rows = per_device * GUESS
    query_local = lax.dynamic_slice_in_dim(query_grid, row_start, local_rows, 0).reshape(
        per_device, GUESS, kv_heads, group, HD
    )
    suf_keys = suffix_keys.reshape(per_device, suf_dev, kv_heads, HD)
    suf_values = suffix_values.reshape(per_device, suf_dev, kv_heads, HD)
    scores = (
        jnp.einsum("rtkgd,rskd->rtkgs", query_local, suf_keys, preferred_element_type=jnp.float32)
        * scale
    )
    visible = (jnp.arange(suf_dev, dtype=jnp.int32)[None, :] < live[:, None])[
        :, None, None, None, :
    ]
    suffix_part = masked_stats(scores, visible, suf_values)
    key_local = lax.dynamic_slice_in_dim(key_new, row_start, local_rows, 0).reshape(
        per_device, GUESS, kv_heads, HD
    )
    value_local = lax.dynamic_slice_in_dim(value_new, row_start, local_rows, 0).reshape(
        per_device, GUESS, kv_heads, HD
    )
    new_scores = (
        jnp.einsum("rtkgd,rskd->rtkgs", query_local, key_local, preferred_element_type=jnp.float32)
        * scale
    )
    guess_ids = jnp.arange(GUESS, dtype=jnp.int32)
    causal = (guess_ids[None, :] <= guess_ids[:, None]) & (seq_index == 0)
    guess_part = masked_stats(new_scores, causal[None, :, None, None, :], value_local)
    prefix_local = (
        lax.dynamic_slice_in_dim(peak_all, row_start, local_rows, 0).reshape(
            per_device, GUESS, kv_heads, group
        ),
        lax.dynamic_slice_in_dim(total_all, row_start, local_rows, 0).reshape(
            per_device, GUESS, kv_heads, group
        ),
        lax.dynamic_slice_in_dim(numer_all, row_start, local_rows, 0).reshape(
            per_device, GUESS, kv_heads, group, HD
        ),
    )
    peak_loc, total_loc, numer_loc = combine(combine(prefix_local, suffix_part), guess_part)
    peak_all = lax.dynamic_update_slice_in_dim(
        peak_all, peak_loc.reshape(local_rows, kv_heads, group), row_start, 0
    )
    total_all = lax.dynamic_update_slice_in_dim(
        total_all, total_loc.reshape(local_rows, kv_heads, group), row_start, 0
    )
    numer_all = lax.dynamic_update_slice_in_dim(
        numer_all, numer_loc.reshape(local_rows, kv_heads, group, HD), row_start, 0
    )
    peaks, totals, numers = (
        lax.all_to_all(peak_all[None], ("roll", "seq"), split_axis=1, concat_axis=0, tiled=True),
        lax.all_to_all(total_all[None], ("roll", "seq"), split_axis=1, concat_axis=0, tiled=True),
        lax.all_to_all(numer_all[None], ("roll", "seq"), split_axis=1, concat_axis=0, tiled=True),
    )
    peak_top = jnp.max(peaks, axis=0)
    factors = jnp.exp(peaks - peak_top[None])
    share = (
        jnp.sum(numers * factors[..., None], axis=0) / jnp.sum(totals * factors, axis=0)[..., None]
    )
    share = share.astype(jnp.bfloat16).reshape(share.shape[0], q_heads * HD)
    attention = lax.all_gather(share, ("roll", "seq"), axis=0, tiled=True)
    summed = lax.psum_scatter(
        jnp.dot(attention, w_out, preferred_element_type=jnp.float32),
        "tp",
        scatter_dimension=0,
        tiled=True,
    )
    return summed.astype(jnp.bfloat16)


SEND_LIMIT = 12 << 20
LOG2E = 1.4426950408889634


def contract_last(a, b):
    return lax.dot_general(a, b, (((1,), (1,)), ((), ())), preferred_element_type=jnp.float32)


def place(out_ref, part, at, block):
    zone = lax.axis_index("roll")
    roll, _, _, width = out_ref.shape
    j, at = at // width, at % width
    for b in range(roll):
        out_ref[b ^ zone, j, :, at : at + part.shape[1]] = part[b * block : (b + 1) * block]


def place_all(x, weights, out_ref, ready):
    *wq, wk, wv = weights
    _, kh, block, width = out_ref.shape
    chunks = len(wq)
    span = wq[0].shape[1]
    wide = width - 2 * HD
    for c in range(chunks):
        ready(c)
        part = jnp.dot(x, wq[c][...], preferred_element_type=jnp.float32)
        place(out_ref, part, c * span // wide * width + c * span % wide, block)
    for c, w, at in ((chunks, wk, wide), (chunks + 1, wv, wide + HD)):
        ready(c)
        part = jnp.dot(x, w[...], preferred_element_type=jnp.float32)
        for j in range(kh):
            place(out_ref, part[:, j * HD : (j + 1) * HD], j * width + at, block)


def project_kernel(x_ref, wq_ref, wk_ref, wv_ref, send_ref, keep_ref, x_all, *refs):
    seq = lax.axis_index("seq")
    sems = refs[-1]
    count = len(refs) // 2
    sources = [wq_ref] * (count - 2) + [wk_ref, wv_ref]

    def copies(half, targets, at):
        made = []
        for n, (source, target) in enumerate(zip(sources, targets)):
            span = target.shape[1]
            start = half * (source.shape[1] // 2) + (n * span if n < count - 2 else 0)
            part = source.at[:, pl.ds(pl.multiple_of(start, span), span)]
            made.append(pltpu.make_async_copy(part, target, sems.at[at + n]))
        return made

    fetch = pltpu.make_async_copy(x_ref, x_all, sems.at[2 * count])
    fetch.start()
    work = []
    for half, out_ref, at in ((1 - seq, send_ref, 0), (seq, keep_ref, count)):
        targets = refs[at : at + count]
        started = copies(half, targets, at)
        for copy in started:
            copy.start()
        work.append((targets, out_ref, started))
    fetch.wait()
    for targets, out_ref, started in work:
        place_all(x_all[...], targets, out_ref, lambda c: started[c].wait())


def project(hidden, w_query, w_key, w_value, roll, kh):
    rows, depth = hidden.shape
    kv_heads = w_key.shape[1] // HD
    wide = w_query.shape[1] // kv_heads
    block = rows // roll
    width = wide + 2 * HD
    span = min(wide, 512)
    chunks = kh * wide // span
    hbm = pl.BlockSpec(memory_space=pltpu.HBM)
    vmem = pl.BlockSpec(memory_space=pltpu.VMEM)
    shapes = ([(depth, span)] * chunks + [(depth, kh * HD)] * 2) * 2
    out = jax.ShapeDtypeStruct((roll, kh, block, width), jnp.float32)
    return pl.pallas_call(
        project_kernel,
        out_shape=[out, out],
        in_specs=[hbm] * 4,
        out_specs=[vmem, vmem],
        scratch_shapes=[pltpu.VMEM((rows, depth), jnp.bfloat16)]
        + [pltpu.VMEM(s, jnp.bfloat16) for s in shapes]
        + [pltpu.SemaphoreType.DMA((len(shapes) + 1,))],
        compiler_params=pltpu.CompilerParams(vmem_limit_bytes=SEND_LIMIT),
        cost_estimate=pl.CostEstimate(
            flops=4 * rows * depth * width * kh, bytes_accessed=4 * depth * width * kh, transcendentals=0
        ),
        name="project",
    )(*[pltpu.with_memory_space_constraint(a, pltpu.HBM) for a in (hidden, w_query, w_key, w_value)])


def finish_kernel(group, per, kh, *refs):
    bq_ref, bk_ref, bv_ref, cos_ref, sin_ref, q_ref, k_ref, v_ref = refs[-8:]
    sums = refs[:-8]
    block = sums[0].shape[1]
    guess = block // per
    seq = lax.axis_index("seq")
    rows = pl.ds(pl.multiple_of(lax.axis_index("roll") * block, block), block)
    cosine = cos_ref[rows, :]
    sine = sin_ref[rows, :]

    def bias_of(ref, n):
        at = seq * (ref.shape[1] // 2) + n * HD
        return ref[:, pl.ds(pl.multiple_of(at, HD), HD)]

    def total(j, g):
        at = slice(g * HD, (g + 1) * HD)
        u = sums[0][j, :, at]
        for o in sums[1:]:
            u = u + o[j, :, at]
        if g < group:
            bias = bias_of(bq_ref, j * group + g)
        else:
            bias = bias_of(bk_ref if g == group else bv_ref, j)
        return u + bias.astype(jnp.float32)

    def turn(u):
        return u * cosine + pltpu.roll(u, HD // 2, 1) * sine

    for j in range(kh):
        for g in range(0, group, 2):
            one = turn(total(j, g))
            two = turn(total(j, g + 1))
            for i in range(per):
                span = slice(i * guess, (i + 1) * guess)
                both = jnp.concatenate([one[span], two[span]], axis=0)
                q_ref[i, j, g * guess : (g + 2) * guess, :] = both.astype(jnp.bfloat16)
        k_ref[j] = turn(total(j, group)).astype(jnp.bfloat16)
        v_ref[j] = total(j, group + 1).astype(jnp.bfloat16)


def finish(sums, biases, cosine, sine, per):
    kh, block, width = sums[0].shape
    group = width // HD - 2
    guess = block // per
    vmem = pl.BlockSpec(memory_space=pltpu.VMEM)
    return pl.pallas_call(
        functools.partial(finish_kernel, group, per, kh),
        in_specs=[vmem] * (len(sums) + len(biases) + 2),
        out_specs=[vmem] * 3,
        out_shape=(
            jax.ShapeDtypeStruct((per, kh, group * guess, HD), jnp.bfloat16),
            jax.ShapeDtypeStruct((kh, block, HD), jnp.bfloat16),
            jax.ShapeDtypeStruct((kh, block, HD), jnp.bfloat16),
        ),
        compiler_params=pltpu.CompilerParams(vmem_limit_bytes=16 << 20),
        name="finish",
    )(*sums, *biases, cosine, sine)


def own_kernel(scale, guess, lengths, q_ref, kn_ref, vn_ref, k0_ref, k1_ref, v0_ref, v1_ref, n_ref, m_ref, l_ref):
    per, kh, width, _ = q_ref.shape
    span = k0_ref.shape[1]
    seq = lax.axis_index("seq")
    zone = lax.axis_index("roll")
    fresh = kn_ref.shape[1]
    key_id = lax.broadcasted_iota(jnp.int32, (width, span), 1)
    new_id = lax.broadcasted_iota(jnp.int32, (width, fresh), 1)
    row_id = lax.broadcasted_iota(jnp.int32, (width, fresh), 0) % guess
    for i in range(per):
        length = lengths[zone * per + i]
        sees = (key_id < length - seq * span, key_id < length - (1 - seq) * span)
        causal = (new_id >= i * guess) & (new_id - i * guess <= row_id)
        sees = sees + (causal,)
        for j in range(kh):
            q = q_ref[i, j]
            at = pl.ds(pl.multiple_of((seq * kh + j) * HD, HD), HD)
            keys = (k0_ref[i, :, at], k1_ref[i, :, at], kn_ref[j])
            values = (v0_ref[i, :, at], v1_ref[i, :, at], vn_ref[j])
            scores = [jnp.where(see, contract_last(q, k), NEG_FILL) for k, see in zip(keys, sees)]
            peak = jnp.max(scores[0], axis=1, keepdims=True)
            for s in scores[1:]:
                peak = jnp.maximum(peak, jnp.max(s, axis=1, keepdims=True))
            total = jnp.zeros((width, 1), jnp.float32)
            numer = jnp.zeros((width, HD), jnp.float32)
            for s, v in zip(scores, values):
                w = jnp.exp2((s - peak) * (scale * LOG2E))
                total = total + jnp.sum(w, axis=1, keepdims=True)
                numer = numer + jnp.dot(w.astype(jnp.bfloat16), v, preferred_element_type=jnp.float32)
            peak = peak * scale
            n_ref[i, j] = numer
            m_ref[i, j] = jnp.broadcast_to(peak, (width, HD))
            l_ref[i, j] = jnp.broadcast_to(total, (width, HD))


def own_attention(lengths, q, k_new, v_new, keys, keys_got, values, values_got, scale, guess):
    per, kh, width, _ = q.shape
    span = keys.shape[1]
    vmem = pl.BlockSpec(memory_space=pltpu.VMEM)
    out = jax.ShapeDtypeStruct(q.shape, jnp.float32)
    elements = per * kh * width * span * 2
    return pl.pallas_call(
        functools.partial(own_kernel, scale, guess),
        in_specs=[pl.BlockSpec(memory_space=pltpu.SMEM)] + [vmem] * 7,
        out_specs=[vmem] * 3,
        out_shape=(out, out, out),
        compiler_params=pltpu.CompilerParams(vmem_limit_bytes=12 << 20),
        cost_estimate=pl.CostEstimate(
            flops=4 * elements * HD, bytes_accessed=8 * per * span * kh * HD, transcendentals=elements
        ),
        name="own_attention",
    )(lengths, q, k_new, v_new, keys, keys_got, values, values_got)


def split_three(x):
    high = x.astype(jnp.bfloat16).astype(jnp.float32)
    rest = x - high
    middle = rest.astype(jnp.bfloat16).astype(jnp.float32)
    return high, middle, rest - middle


def prefix_kernel(scale, roll, prompts, *refs):
    q_refs = refs[:roll]
    k0_ref, k1_ref, v0_ref, v1_ref, on_ref, om_ref, ol_ref = refs[roll : roll + 7]
    n_out, m_out, l_out = refs[roll + 7 : roll + 10]
    packed = refs[roll + 10 : 2 * roll + 9]
    q_all, n_all, m_all, l_all, order = refs[2 * roll + 9 :]
    per, kh, width, _ = q_refs[0].shape
    zone = lax.axis_index("roll")
    seq = lax.axis_index("seq")
    count = k0_ref.shape[0]
    share = roll * per // count

    for k in range(roll):
        q_all[k * per : (k + 1) * per] = q_refs[k][...]
    filled = [jnp.int32(p * share) for p in range(count)]
    for k in range(roll):
        for i in range(per):
            owner = prompts[(zone ^ k) * per + i]
            for p in range(count):
                chosen = owner == p

                @pl.when(chosen)
                def _():
                    order[filled[p]] = k * per + i

                filled[p] = filled[p] + chosen.astype(jnp.int32)

    for p in range(count):
        ids = [order[p * share + n] for n in range(share)]
        for j in range(kh):
            at = pl.ds(pl.multiple_of((seq * kh + j) * HD, HD), HD)
            q = jnp.concatenate([q_all[n, j] for n in ids], axis=0)
            scores = [contract_last(q, k_ref[p, :, at]) for k_ref in (k0_ref, k1_ref)]
            peak = jnp.maximum(
                jnp.max(scores[0], axis=1, keepdims=True), jnp.max(scores[1], axis=1, keepdims=True)
            )
            total = jnp.zeros(peak.shape, jnp.float32)
            numer = jnp.zeros((share * width, HD), jnp.float32)
            for s, v_ref in zip(scores, (v0_ref, v1_ref)):
                w = jnp.exp2((s - peak) * (scale * LOG2E))
                total = total + jnp.sum(w, axis=1, keepdims=True)
                numer = numer + jnp.dot(
                    w.astype(jnp.bfloat16), v_ref[p, :, at], preferred_element_type=jnp.float32
                )
            peak = jnp.broadcast_to(peak * scale, numer.shape)
            total = jnp.broadcast_to(total, numer.shape)
            for n, to in enumerate(ids):
                span = slice(n * width, (n + 1) * width)
                n_all[to, j] = numer[span]
                m_all[to, j] = peak[span]
                l_all[to, j] = total[span]

    for i in range(per):
        for h in range(kh):
            m_a, m_b = m_all[i, h], om_ref[i, h]
            peak = jnp.maximum(m_a, m_b)
            f_a, f_b = jnp.exp(m_a - peak), jnp.exp(m_b - peak)
            m_out[i, h] = peak
            l_out[i, h] = l_all[i, h] * f_a + ol_ref[i, h] * f_b
            n_out[i, h] = n_all[i, h] * f_a + on_ref[i, h] * f_b
    lane = lax.broadcasted_iota(jnp.int32, (width, HD), 1)
    for k in range(1, roll):
        stats = jnp.zeros((width, HD), jnp.float32)
        for i in range(per):
            for h in range(kh):
                u = i * kh + h
                packed[k - 1][u * width : (u + 1) * width, :] = n_all[k * per + i, h].astype(jnp.bfloat16)
                pieces = split_three(m_all[k * per + i, h]) + split_three(l_all[k * per + i, h])
                for c, piece in enumerate(pieces):
                    stats = jnp.where(lane == 6 * u + c, piece, stats)
        u = per * kh
        packed[k - 1][u * width : (u + 1) * width, :] = stats.astype(jnp.bfloat16)


def prefix_attention(prompt_of, queries, keys, keys_got, values, values_got, own, scale):
    roll = len(queries)
    per, kh, width, _ = queries[0].shape
    prompts, span, _ = keys.shape
    vmem = pl.BlockSpec(memory_space=pltpu.VMEM)
    rows = (per * kh + 1) * width
    out = jax.ShapeDtypeStruct(queries[0].shape, jnp.float32)
    elements = roll * per * kh * width * span * 2
    everything = (roll * per, kh, width, HD)
    outs = pl.pallas_call(
        functools.partial(prefix_kernel, scale, roll),
        in_specs=[pl.BlockSpec(memory_space=pltpu.SMEM)] + [vmem] * (roll + 7),
        out_specs=[vmem] * (roll + 2),
        scratch_shapes=[pltpu.VMEM(everything, jnp.bfloat16)]
        + [pltpu.VMEM(everything, jnp.float32)] * 3
        + [pltpu.SMEM((roll * per,), jnp.int32)],
        out_shape=[out] * 3 + [jax.ShapeDtypeStruct((rows, HD), jnp.bfloat16)] * (roll - 1),
        compiler_params=pltpu.CompilerParams(vmem_limit_bytes=12 << 20),
        cost_estimate=pl.CostEstimate(
            flops=4 * elements * HD, bytes_accessed=8 * prompts * span * kh * HD, transcendentals=elements
        ),
        name="prefix_attention",
    )(prompt_of, *queries, keys, keys_got, values, values_got, *own)
    return outs[:3], outs[3:]


def merge_kernel(group, n_ref, m_ref, l_ref, *refs):
    packed, out_ref = refs[:-1], refs[-1]
    per, kh, width, _ = n_ref.shape
    guess = width // group
    stats = [p[per * kh * width :, :].astype(jnp.float32) for p in packed]
    results = {}
    for i in range(per):
        for h in range(kh):
            u = i * kh + h

            def column(s, c):
                c = 6 * u + c
                return s[:, c : c + 1] + s[:, c + 1 : c + 2] + s[:, c + 2 : c + 3]

            peaks = [m_ref[i, h]] + [jnp.broadcast_to(column(s, 0), (width, HD)) for s in stats]
            totals = [l_ref[i, h]] + [jnp.broadcast_to(column(s, 3), (width, HD)) for s in stats]
            numers = [n_ref[i, h]] + [p[u * width : (u + 1) * width, :].astype(jnp.float32) for p in packed]
            top = functools.reduce(jnp.maximum, peaks)
            total = jnp.zeros((width, HD), jnp.float32)
            numer = jnp.zeros((width, HD), jnp.float32)
            for m, l, n in zip(peaks, totals, numers):
                f = jnp.exp(m - top)
                total = total + l * f
                numer = numer + n * f
            results[i, h] = numer / total
    for h in range(kh):
        for g in range(group):
            rows = [results[i, h][g * guess : (g + 1) * guess] for i in range(per)]
            at = (h * group + g) * HD
            out_ref[:, at : at + HD] = jnp.concatenate(rows, axis=0).astype(jnp.bfloat16)


def merge(own, packed, group):
    per, kh, width, _ = own[0].shape
    whole = pl.BlockSpec(own[0].shape, lambda n: (0, 0, 0, 0))
    sent = pl.BlockSpec(packed[0].shape, lambda n: (0, 0))
    shape = (per * width // group, kh * group * HD)
    return pl.pallas_call(
        functools.partial(merge_kernel, group),
        grid=(1,),
        out_shape=jax.ShapeDtypeStruct(shape, jnp.bfloat16),
        in_specs=[whole] * 3 + [sent] * len(packed),
        out_specs=pl.BlockSpec(shape, lambda n: (0, 0)),
        compiler_params=pltpu.CompilerParams(vmem_limit_bytes=16 << 20),
        name="merge",
    )(*own, *packed)


def output_kernel(roll, theirs, *refs):
    parts, w_ref, rest = refs[:roll], refs[roll], refs[roll + 1 :]
    lhs = rest[-1]
    zone, seq, tp = lax.axis_index("roll"), lax.axis_index("seq"), lax.axis_index("tp")
    block, cols = parts[0].shape
    side = 1 - seq if theirs else seq
    for k in range(roll):
        at = pl.multiple_of((zone ^ k ^ (tp * (roll // 2))) * block, block)
        lhs[pl.ds(at, block), :] = parts[k][...]
    w = w_ref[pl.ds(pl.multiple_of(side * cols, cols), cols), :]
    part = jnp.dot(lhs[...], w, preferred_element_type=jnp.float32)
    if not theirs:
        rest[0][...] = part
        return
    part = rest[0][...] + part
    keep_ref, send_ref = rest[1:3]
    rows = keep_ref.shape[0]
    keep_ref[...] = part[:rows]
    send_ref[...] = part[rows:].astype(send_ref.dtype)


def output(parts, w_out, before=None):
    roll = len(parts)
    block, cols = parts[0].shape
    width = w_out.shape[1]
    rows = roll * block
    vmem = pl.BlockSpec(memory_space=pltpu.VMEM)
    theirs = before is not None
    if theirs:
        shapes = [
            jax.ShapeDtypeStruct((rows // 2, width), jnp.float32),
            jax.ShapeDtypeStruct((rows // 2, width), jnp.bfloat16),
        ]
    else:
        shapes = jax.ShapeDtypeStruct((rows, width), jnp.float32)
    return pl.pallas_call(
        functools.partial(output_kernel, roll, theirs),
        in_specs=[vmem] * (roll + 1 + theirs),
        out_specs=[vmem, vmem] if theirs else vmem,
        scratch_shapes=[pltpu.VMEM((rows, cols), jnp.bfloat16)],
        out_shape=shapes,
        compiler_params=pltpu.CompilerParams(vmem_limit_bytes=16 << 20),
        cost_estimate=pl.CostEstimate(
            flops=2 * rows * cols * width, bytes_accessed=2 * cols * width, transcendentals=0
        ),
        name="output_theirs" if theirs else "output_mine",
    )(*parts, w_out, *((before,) if theirs else ()))


def fast_body(
    hidden,
    w_query,
    w_key,
    w_value,
    b_query,
    b_key,
    b_value,
    w_out,
    prefix_keys,
    prefix_values,
    suffix_keys,
    suffix_values,
    suffix_lengths,
    prompt_of,
):
    roll = lax.axis_size("roll")
    kv_heads = w_key.shape[1] // HD
    group = w_query.shape[1] // w_key.shape[1]
    kh = kv_heads // 2
    per = suffix_keys.shape[0]
    block = hidden.shape[0] // roll
    guess = block // per
    scale = 1.0 / math.sqrt(HD)

    def across(x):
        return lax.ppermute(x, "seq", [(0, 1), (1, 0)])

    def hop(x, k):
        return lax.ppermute(x, "roll", [(n, n ^ k) for n in range(roll)])

    def hops(pick):
        sent = {k: hop(pick(k), k) for k in reversed(range(1, roll))}
        return [sent[k] for k in range(1, roll)]

    send, keep = project(hidden, w_query, w_key, w_value, roll, kh)
    got = across(send)
    terms = [keep[k] + got[k] for k in range(roll)]
    sums = [terms[0]] + hops(lambda k: terms[k])
    caches = (suffix_keys, suffix_values, prefix_keys, prefix_values)
    _, small = lax.optimization_barrier(
        (terms[0], (suffix_lengths, b_query, b_key, b_value, *caches))
    )
    caches = small[4:]

    sk_got, sv_got, pk_got, pv_got = [across(x) for x in caches]

    row_ids = jnp.arange(hidden.shape[0], dtype=jnp.int32)
    prefix_total = prefix_keys.shape[1] * roll * 2
    positions = (prefix_total + lookup(small[0], row_ids // guess) + row_ids % guess).astype(jnp.float32)
    half = HD // 2
    steps = jnp.arange(half).astype(jnp.float32) * (2.0 / HD)
    freqs = jnp.exp(-math.log(ROPE_BASE) * steps)
    angles = positions[:, None] * freqs[None, :]
    cosine = jnp.cos(angles)
    sine = jnp.sin(angles)
    cosine = jnp.concatenate([cosine, cosine], axis=-1)
    sine = jnp.concatenate([-sine, sine], axis=-1)
    biases = [b[None, :] for b in small[1:4]]

    q, k_new, v_new = finish(sums, biases, cosine, sine, per)
    queries = [q] + hops(lambda k: q)
    own = own_attention(
        suffix_lengths, q, k_new, v_new, suffix_keys, sk_got, suffix_values, sv_got, scale, guess
    )
    own, packed = prefix_attention(
        prompt_of, queries, prefix_keys, pk_got, prefix_values, pv_got, own, scale
    )
    packed = hops(lambda k: packed[k - 1])
    share = merge(own, packed, group)
    mine = [share] + hops(lambda k: share)
    theirs = [across(m) for m in mine]
    kept, sent = output(theirs, w_out, output(mine, w_out))
    arrived = lax.ppermute(sent, "tp", [(0, 1), (1, 0)])
    return (kept + arrived.astype(jnp.float32)).astype(jnp.bfloat16)


def body(*arrays):
    hidden, w_key, prompt_of, suffix_keys = arrays[0], arrays[2], arrays[13], arrays[10]
    roll = lax.axis_size("roll")
    block = hidden.shape[0] // roll
    fits = (
        lax.axis_size("seq") == 2
        and lax.axis_size("tp") == 2
        and roll & (roll - 1) == 0
        and (w_key.shape[1] // HD) % 2 == 0
        and block % 16 == 0
        and block == suffix_keys.shape[0] * GUESS
        and 6 * suffix_keys.shape[0] * (w_key.shape[1] // HD) <= 2 * HD
        and prompt_of.shape[0] % arrays[8].shape[0] == 0
    )
    if not fits:
        return general_body(*arrays)
    return fast_body(*arrays)


def solution(mesh):
    return jax.shard_map(
        body,
        mesh=mesh,
        in_specs=(
            P("groups", ("roll", "seq")),
            P(("roll", "seq"), "tp"),
            P(("roll", "seq"), "tp"),
            P(("roll", "seq"), "tp"),
            P("tp"),
            P("tp"),
            P("tp"),
            P("tp", ("roll", "seq")),
            P("groups", ("roll", "seq"), "tp"),
            P("groups", ("roll", "seq"), "tp"),
            P(("groups", "roll"), "seq", "tp"),
            P(("groups", "roll"), "seq", "tp"),
            P("groups"),
            P("groups"),
        ),
        out_specs=P(("groups", "tp"), ("roll", "seq")),
        check_vma=False,
    )
```

```python
import functools
import math

import jax
import jax.numpy as jnp
from jax import lax
from jax.experimental import pallas as pl
from jax.experimental.pallas import tpu as pltpu
from jax.sharding import PartitionSpec as P


HD = 128
GUESS = 8


ROPE_BASE = 1000000.0
NEG_FILL = -1e30


def rotate(values, positions):
    half = values.shape[-1] // 2
    steps = jnp.arange(half).astype(jnp.float32) * (2.0 / values.shape[-1])
    freqs = jnp.exp(-math.log(ROPE_BASE) * steps)
    angles = positions[:, None] * freqs[None, :]
    cosine = jnp.cos(angles)[:, None, :]
    sine = jnp.sin(angles)[:, None, :]
    first = values[..., :half]
    second = values[..., half:]
    return jnp.concatenate(
        [first * cosine - second * sine, second * cosine + first * sine], axis=-1
    )


def lookup(table, indices):
    hits = indices[:, None] == jnp.arange(table.shape[0], dtype=jnp.int32)[None, :]
    return jnp.sum(jnp.where(hits, table[None, :], 0), axis=1)


def combine(first, second):
    peak_a, total_a, numer_a = first
    peak_b, total_b, numer_b = second
    peak = jnp.maximum(peak_a, peak_b)
    factor_a = jnp.exp(peak_a - peak)
    factor_b = jnp.exp(peak_b - peak)
    return (
        peak,
        total_a * factor_a + total_b * factor_b,
        numer_a * factor_a[..., None] + numer_b * factor_b[..., None],
    )


def masked_stats(scores, visible, values):
    peak = jnp.max(jnp.where(visible, scores, NEG_FILL), axis=-1)
    weights = jnp.exp(jnp.where(visible, scores - peak[..., None], NEG_FILL))
    total = jnp.sum(weights, axis=-1)
    numer = jnp.einsum(
        "rtkgs,rskd->rtkgd",
        weights.astype(jnp.bfloat16),
        values,
        preferred_element_type=jnp.float32,
    )
    return (peak, total, numer)


def general_body(
    hidden,
    w_query,
    w_key,
    w_value,
    b_query,
    b_key,
    b_value,
    w_out,
    prefix_keys,
    prefix_values,
    suffix_keys,
    suffix_values,
    suffix_lengths,
    prompt_of,
):
    row_count = hidden.shape[0]
    q_heads = w_query.shape[1] // HD
    kv_heads = w_key.shape[1] // HD
    group = q_heads // kv_heads
    prompts = prefix_keys.shape[0]
    pre_dev = prefix_keys.shape[1]
    prefix_total = pre_dev * lax.axis_size(("roll", "seq"))
    per_device = suffix_keys.shape[0]
    suf_dev = suffix_keys.shape[1]
    scale = 1.0 / math.sqrt(HD)
    q_part = jnp.dot(hidden, w_query, preferred_element_type=jnp.float32)
    k_part = jnp.dot(hidden, w_key, preferred_element_type=jnp.float32)
    v_part = jnp.dot(hidden, w_value, preferred_element_type=jnp.float32)
    q_sum, k_sum, v_sum = lax.psum((q_part, k_part, v_part), ("roll", "seq"))
    count = q_sum.shape[0]
    row_ids = jnp.arange(count, dtype=jnp.int32)
    owner_ids = row_ids // GUESS
    positions = (prefix_total + lookup(suffix_lengths, owner_ids) + row_ids % GUESS).astype(
        jnp.float32
    )
    q_rot = rotate((q_sum + b_query.astype(jnp.float32)).reshape(count, q_heads, HD), positions)
    k_rot = rotate((k_sum + b_key.astype(jnp.float32)).reshape(count, kv_heads, HD), positions)
    v_fin = (v_sum + b_value.astype(jnp.float32)).reshape(count, kv_heads, HD)
    query = q_rot.astype(jnp.bfloat16)
    key_new = k_rot.astype(jnp.bfloat16)
    value_new = v_fin.astype(jnp.bfloat16)
    query_grid = query.reshape(row_count, kv_heads, group, HD)
    owners_all = jnp.arange(row_count, dtype=jnp.int32) // GUESS
    row_prompt = lookup(prompt_of, owners_all)
    pre_keys = prefix_keys.reshape(prompts, pre_dev, kv_heads, HD)
    pre_values = prefix_values.reshape(prompts, pre_dev, kv_heads, HD)
    peak_all = jnp.full((row_count, kv_heads, group), NEG_FILL, jnp.float32)
    total_all = jnp.zeros((row_count, kv_heads, group), jnp.float32)
    numer_all = jnp.zeros((row_count, kv_heads, group, HD), jnp.float32)
    for prompt in range(prompts):
        scores = (
            jnp.einsum(
                "tkgd,skd->tkgs", query_grid, pre_keys[prompt], preferred_element_type=jnp.float32
            )
            * scale
        )
        block_peak = jnp.max(scores, axis=-1)
        weights = jnp.exp(scores - block_peak[..., None])
        block_numer = jnp.einsum(
            "tkgs,skd->tkgd",
            weights.astype(jnp.bfloat16),
            pre_values[prompt],
            preferred_element_type=jnp.float32,
        )
        picked = (row_prompt == prompt)[:, None, None]
        peak_all = jnp.where(picked, block_peak, peak_all)
        total_all = jnp.where(picked, jnp.sum(weights, axis=-1), total_all)
        numer_all = jnp.where(picked[..., None], block_numer, numer_all)
    first_rollout = lax.axis_index("roll") * per_device
    seq_index = lax.axis_index("seq")
    local_len = lax.dynamic_slice_in_dim(suffix_lengths, first_rollout, per_device, 0)
    live = jnp.clip(local_len - seq_index * suf_dev, 0, suf_dev)
    row_start = first_rollout * GUESS
    local_rows = per_device * GUESS
    query_local = lax.dynamic_slice_in_dim(query_grid, row_start, local_rows, 0).reshape(
        per_device, GUESS, kv_heads, group, HD
    )
    suf_keys = suffix_keys.reshape(per_device, suf_dev, kv_heads, HD)
    suf_values = suffix_values.reshape(per_device, suf_dev, kv_heads, HD)
    scores = (
        jnp.einsum("rtkgd,rskd->rtkgs", query_local, suf_keys, preferred_element_type=jnp.float32)
        * scale
    )
    visible = (jnp.arange(suf_dev, dtype=jnp.int32)[None, :] < live[:, None])[
        :, None, None, None, :
    ]
    suffix_part = masked_stats(scores, visible, suf_values)
    key_local = lax.dynamic_slice_in_dim(key_new, row_start, local_rows, 0).reshape(
        per_device, GUESS, kv_heads, HD
    )
    value_local = lax.dynamic_slice_in_dim(value_new, row_start, local_rows, 0).reshape(
        per_device, GUESS, kv_heads, HD
    )
    new_scores = (
        jnp.einsum("rtkgd,rskd->rtkgs", query_local, key_local, preferred_element_type=jnp.float32)
        * scale
    )
    guess_ids = jnp.arange(GUESS, dtype=jnp.int32)
    causal = (guess_ids[None, :] <= guess_ids[:, None]) & (seq_index == 0)
    guess_part = masked_stats(new_scores, causal[None, :, None, None, :], value_local)
    prefix_local = (
        lax.dynamic_slice_in_dim(peak_all, row_start, local_rows, 0).reshape(
            per_device, GUESS, kv_heads, group
        ),
        lax.dynamic_slice_in_dim(total_all, row_start, local_rows, 0).reshape(
            per_device, GUESS, kv_heads, group
        ),
        lax.dynamic_slice_in_dim(numer_all, row_start, local_rows, 0).reshape(
            per_device, GUESS, kv_heads, group, HD
        ),
    )
    peak_loc, total_loc, numer_loc = combine(combine(prefix_local, suffix_part), guess_part)
    peak_all = lax.dynamic_update_slice_in_dim(
        peak_all, peak_loc.reshape(local_rows, kv_heads, group), row_start, 0
    )
    total_all = lax.dynamic_update_slice_in_dim(
        total_all, total_loc.reshape(local_rows, kv_heads, group), row_start, 0
    )
    numer_all = lax.dynamic_update_slice_in_dim(
        numer_all, numer_loc.reshape(local_rows, kv_heads, group, HD), row_start, 0
    )
    peaks, totals, numers = (
        lax.all_to_all(peak_all[None], ("roll", "seq"), split_axis=1, concat_axis=0, tiled=True),
        lax.all_to_all(total_all[None], ("roll", "seq"), split_axis=1, concat_axis=0, tiled=True),
        lax.all_to_all(numer_all[None], ("roll", "seq"), split_axis=1, concat_axis=0, tiled=True),
    )
    peak_top = jnp.max(peaks, axis=0)
    factors = jnp.exp(peaks - peak_top[None])
    share = (
        jnp.sum(numers * factors[..., None], axis=0) / jnp.sum(totals * factors, axis=0)[..., None]
    )
    share = share.astype(jnp.bfloat16).reshape(share.shape[0], q_heads * HD)
    attention = lax.all_gather(share, ("roll", "seq"), axis=0, tiled=True)
    summed = lax.psum_scatter(
        jnp.dot(attention, w_out, preferred_element_type=jnp.float32),
        "tp",
        scatter_dimension=0,
        tiled=True,
    )
    return summed.astype(jnp.bfloat16)


SEND_LIMIT = 12 << 20
LOG2E = 1.4426950408889634


def contract_last(a, b):
    return lax.dot_general(a, b, (((1,), (1,)), ((), ())), preferred_element_type=jnp.float32)


def place(out_ref, part, at, block):
    zone = lax.axis_index("roll")
    roll, _, _, width = out_ref.shape
    j, at = at // width, at % width
    for b in range(roll):
        out_ref[b ^ zone, j, :, at : at + part.shape[1]] = part[b * block : (b + 1) * block]


def place_all(x, weights, out_ref, ready):
    *wq, wk, wv = weights
    _, kh, block, width = out_ref.shape
    chunks = len(wq)
    span = wq[0].shape[1]
    wide = width - 2 * HD
    for c in range(chunks):
        ready(c)
        part = jnp.dot(x, wq[c][...], preferred_element_type=jnp.float32)
        place(out_ref, part, c * span // wide * width + c * span % wide, block)
    for c, w, at in ((chunks, wk, wide), (chunks + 1, wv, wide + HD)):
        ready(c)
        part = jnp.dot(x, w[...], preferred_element_type=jnp.float32)
        for j in range(kh):
            place(out_ref, part[:, j * HD : (j + 1) * HD], j * width + at, block)


def project_kernel(x_ref, wq_ref, wk_ref, wv_ref, send_ref, keep_ref, x_all, *refs):
    seq = lax.axis_index("seq")
    sems = refs[-1]
    count = len(refs) // 2
    sources = [wq_ref] * (count - 2) + [wk_ref, wv_ref]

    def copies(half, targets, at):
        made = []
        for n, (source, target) in enumerate(zip(sources, targets)):
            span = target.shape[1]
            start = half * (source.shape[1] // 2) + (n * span if n < count - 2 else 0)
            part = source.at[:, pl.ds(pl.multiple_of(start, span), span)]
            made.append(pltpu.make_async_copy(part, target, sems.at[at + n]))
        return made

    fetch = pltpu.make_async_copy(x_ref, x_all, sems.at[2 * count])
    fetch.start()
    work = []
    for half, out_ref, at in ((1 - seq, send_ref, 0), (seq, keep_ref, count)):
        targets = refs[at : at + count]
        started = copies(half, targets, at)
        for copy in started:
            copy.start()
        work.append((targets, out_ref, started))
    fetch.wait()
    for targets, out_ref, started in work:
        place_all(x_all[...], targets, out_ref, lambda c: started[c].wait())


def project(hidden, w_query, w_key, w_value, roll, kh):
    rows, depth = hidden.shape
    kv_heads = w_key.shape[1] // HD
    wide = w_query.shape[1] // kv_heads
    block = rows // roll
    width = wide + 2 * HD
    span = min(wide, 512)
    chunks = kh * wide // span
    hbm = pl.BlockSpec(memory_space=pltpu.HBM)
    vmem = pl.BlockSpec(memory_space=pltpu.VMEM)
    shapes = ([(depth, span)] * chunks + [(depth, kh * HD)] * 2) * 2
    out = jax.ShapeDtypeStruct((roll, kh, block, width), jnp.float32)
    return pl.pallas_call(
        project_kernel,
        out_shape=[out, out],
        in_specs=[hbm] * 4,
        out_specs=[vmem, vmem],
        scratch_shapes=[pltpu.VMEM((rows, depth), jnp.bfloat16)]
        + [pltpu.VMEM(s, jnp.bfloat16) for s in shapes]
        + [pltpu.SemaphoreType.DMA((len(shapes) + 1,))],
        compiler_params=pltpu.CompilerParams(vmem_limit_bytes=SEND_LIMIT),
        cost_estimate=pl.CostEstimate(
            flops=4 * rows * depth * width * kh, bytes_accessed=4 * depth * width * kh, transcendentals=0
        ),
        name="project",
    )(*[pltpu.with_memory_space_constraint(a, pltpu.HBM) for a in (hidden, w_query, w_key, w_value)])


def finish_kernel(group, per, kh, *refs):
    bq_ref, bk_ref, bv_ref, cos_ref, sin_ref, q_ref, k_ref, v_ref = refs[-8:]
    sums = refs[:-8]
    block = sums[0].shape[1]
    guess = block // per
    seq = lax.axis_index("seq")
    rows = pl.ds(pl.multiple_of(lax.axis_index("roll") * block, block), block)
    cosine = cos_ref[rows, :]
    sine = sin_ref[rows, :]

    def bias_of(ref, n):
        at = seq * (ref.shape[1] // 2) + n * HD
        return ref[:, pl.ds(pl.multiple_of(at, HD), HD)]

    def total(j, g):
        at = slice(g * HD, (g + 1) * HD)
        u = sums[0][j, :, at]
        for o in sums[1:]:
            u = u + o[j, :, at]
        if g < group:
            bias = bias_of(bq_ref, j * group + g)
        else:
            bias = bias_of(bk_ref if g == group else bv_ref, j)
        return u + bias.astype(jnp.float32)

    def turn(u):
        return u * cosine + pltpu.roll(u, HD // 2, 1) * sine

    for j in range(kh):
        for g in range(0, group, 2):
            one = turn(total(j, g))
            two = turn(total(j, g + 1))
            for i in range(per):
                span = slice(i * guess, (i + 1) * guess)
                both = jnp.concatenate([one[span], two[span]], axis=0)
                q_ref[i, j, g * guess : (g + 2) * guess, :] = both.astype(jnp.bfloat16)
        k_ref[j] = turn(total(j, group)).astype(jnp.bfloat16)
        v_ref[j] = total(j, group + 1).astype(jnp.bfloat16)


def finish(sums, biases, cosine, sine, per):
    kh, block, width = sums[0].shape
    group = width // HD - 2
    guess = block // per
    vmem = pl.BlockSpec(memory_space=pltpu.VMEM)
    return pl.pallas_call(
        functools.partial(finish_kernel, group, per, kh),
        in_specs=[vmem] * (len(sums) + len(biases) + 2),
        out_specs=[vmem] * 3,
        out_shape=(
            jax.ShapeDtypeStruct((per, kh, group * guess, HD), jnp.bfloat16),
            jax.ShapeDtypeStruct((kh, block, HD), jnp.bfloat16),
            jax.ShapeDtypeStruct((kh, block, HD), jnp.bfloat16),
        ),
        compiler_params=pltpu.CompilerParams(vmem_limit_bytes=16 << 20),
        name="finish",
    )(*sums, *biases, cosine, sine)


def fetch_kernel(*refs):
    count = len(refs) // 2
    sems = refs[-1]
    seq = lax.axis_index("seq")
    copies = []
    for n, (source, target) in enumerate(zip(refs[:count], refs[count:-1])):
        cols = target.shape[2]
        part = source.at[:, :, pl.ds(pl.multiple_of(seq * cols, cols), cols)]
        copies.append(pltpu.make_async_copy(part, target, sems.at[n]))
    for copy in copies:
        copy.start()
    for copy in copies:
        copy.wait()


def fetch(caches):
    shapes = [(c.shape[0], c.shape[1], c.shape[2] // 2) for c in caches]
    return pl.pallas_call(
        fetch_kernel,
        in_specs=[pl.BlockSpec(memory_space=pltpu.HBM)] * len(caches),
        out_specs=[pl.BlockSpec(memory_space=pltpu.VMEM)] * len(caches),
        out_shape=[jax.ShapeDtypeStruct(s, jnp.bfloat16) for s in shapes],
        scratch_shapes=[pltpu.SemaphoreType.DMA((len(caches),))],
        compiler_params=pltpu.CompilerParams(vmem_limit_bytes=1 << 20),
        cost_estimate=pl.CostEstimate(
            flops=0, bytes_accessed=2 * sum(math.prod(s) for s in shapes), transcendentals=0
        ),
        name="fetch",
    )(*[pltpu.with_memory_space_constraint(c, pltpu.HBM) for c in caches])


def own_kernel(scale, guess, lengths, q_ref, kn_ref, vn_ref, k0_ref, k1_ref, v0_ref, v1_ref, n_ref, m_ref, l_ref):
    per, kh, width, _ = q_ref.shape
    span = k0_ref.shape[1]
    seq = lax.axis_index("seq")
    zone = lax.axis_index("roll")
    fresh = kn_ref.shape[1]
    key_id = lax.broadcasted_iota(jnp.int32, (width, span), 1)
    new_id = lax.broadcasted_iota(jnp.int32, (width, fresh), 1)
    row_id = lax.broadcasted_iota(jnp.int32, (width, fresh), 0) % guess
    for i in range(per):
        length = lengths[zone * per + i]
        sees = (key_id < length - seq * span, key_id < length - (1 - seq) * span)
        causal = (new_id >= i * guess) & (new_id - i * guess <= row_id)
        sees = sees + (causal,)
        for j in range(kh):
            q = q_ref[i, j]
            at = pl.ds(pl.multiple_of((seq * kh + j) * HD, HD), HD)
            mine = slice(j * HD, (j + 1) * HD)
            keys = (k0_ref[i, :, mine], k1_ref[i, :, at], kn_ref[j])
            values = (v0_ref[i, :, mine], v1_ref[i, :, at], vn_ref[j])
            scores = [jnp.where(see, contract_last(q, k), NEG_FILL) for k, see in zip(keys, sees)]
            peak = jnp.max(scores[0], axis=1, keepdims=True)
            for s in scores[1:]:
                peak = jnp.maximum(peak, jnp.max(s, axis=1, keepdims=True))
            total = jnp.zeros((width, 1), jnp.float32)
            numer = jnp.zeros((width, HD), jnp.float32)
            for s, v in zip(scores, values):
                w = jnp.exp2((s - peak) * (scale * LOG2E))
                total = total + jnp.sum(w, axis=1, keepdims=True)
                numer = numer + jnp.dot(w.astype(jnp.bfloat16), v, preferred_element_type=jnp.float32)
            peak = peak * scale
            n_ref[i, j] = numer
            m_ref[i, j] = jnp.broadcast_to(peak, (width, HD))
            l_ref[i, j] = jnp.broadcast_to(total, (width, HD))


def own_attention(lengths, q, k_new, v_new, keys, keys_got, values, values_got, scale, guess):
    per, kh, width, _ = q.shape
    span = keys.shape[1]
    vmem = pl.BlockSpec(memory_space=pltpu.VMEM)
    out = jax.ShapeDtypeStruct(q.shape, jnp.float32)
    elements = per * kh * width * span * 2
    return pl.pallas_call(
        functools.partial(own_kernel, scale, guess),
        in_specs=[pl.BlockSpec(memory_space=pltpu.SMEM)] + [vmem] * 7,
        out_specs=[vmem] * 3,
        out_shape=(out, out, out),
        compiler_params=pltpu.CompilerParams(vmem_limit_bytes=12 << 20),
        cost_estimate=pl.CostEstimate(
            flops=4 * elements * HD, bytes_accessed=8 * per * span * kh * HD, transcendentals=elements
        ),
        name="own_attention",
    )(lengths, q, k_new, v_new, keys, keys_got, values, values_got)


def split_three(x):
    high = x.astype(jnp.bfloat16).astype(jnp.float32)
    rest = x - high
    middle = rest.astype(jnp.bfloat16).astype(jnp.float32)
    return high, middle, rest - middle


def prefix_kernel(scale, roll, prompts, *refs):
    q_refs = refs[:roll]
    k0_ref, k1_ref, v0_ref, v1_ref, on_ref, om_ref, ol_ref = refs[roll : roll + 7]
    n_out, m_out, l_out = refs[roll + 7 : roll + 10]
    packed = refs[roll + 10 : 2 * roll + 9]
    q_all, n_all, m_all, l_all, order = refs[2 * roll + 9 :]
    per, kh, width, _ = q_refs[0].shape
    zone = lax.axis_index("roll")
    seq = lax.axis_index("seq")
    count = k0_ref.shape[0]
    share = roll * per // count

    for k in range(roll):
        q_all[k * per : (k + 1) * per] = q_refs[k][...]
    filled = [jnp.int32(p * share) for p in range(count)]
    for k in range(roll):
        for i in range(per):
            owner = prompts[(zone ^ k) * per + i]
            for p in range(count):
                chosen = owner == p

                @pl.when(chosen)
                def _():
                    order[filled[p]] = k * per + i

                filled[p] = filled[p] + chosen.astype(jnp.int32)

    for p in range(count):
        ids = [order[p * share + n] for n in range(share)]
        for j in range(kh):
            at = pl.ds(pl.multiple_of((seq * kh + j) * HD, HD), HD)
            q = jnp.concatenate([q_all[n, j] for n in ids], axis=0)
            mine = slice(j * HD, (j + 1) * HD)
            scores = [contract_last(q, k_ref[p, :, to]) for k_ref, to in ((k0_ref, mine), (k1_ref, at))]
            peak = jnp.maximum(
                jnp.max(scores[0], axis=1, keepdims=True), jnp.max(scores[1], axis=1, keepdims=True)
            )
            total = jnp.zeros(peak.shape, jnp.float32)
            numer = jnp.zeros((share * width, HD), jnp.float32)
            for s, v_ref, to in zip(scores, (v0_ref, v1_ref), (mine, at)):
                w = jnp.exp2((s - peak) * (scale * LOG2E))
                total = total + jnp.sum(w, axis=1, keepdims=True)
                numer = numer + jnp.dot(
                    w.astype(jnp.bfloat16), v_ref[p, :, to], preferred_element_type=jnp.float32
                )
            peak = jnp.broadcast_to(peak * scale, numer.shape)
            total = jnp.broadcast_to(total, numer.shape)
            for n, slot in enumerate(ids):
                span = slice(n * width, (n + 1) * width)
                n_all[slot, j] = numer[span]
                m_all[slot, j] = peak[span]
                l_all[slot, j] = total[span]

    for i in range(per):
        for h in range(kh):
            m_a, m_b = m_all[i, h], om_ref[i, h]
            peak = jnp.maximum(m_a, m_b)
            f_a, f_b = jnp.exp(m_a - peak), jnp.exp(m_b - peak)
            m_out[i, h] = peak
            l_out[i, h] = l_all[i, h] * f_a + ol_ref[i, h] * f_b
            n_out[i, h] = n_all[i, h] * f_a + on_ref[i, h] * f_b
    lane = lax.broadcasted_iota(jnp.int32, (width, HD), 1)
    for k in range(1, roll):
        stats = jnp.zeros((width, HD), jnp.float32)
        for i in range(per):
            for h in range(kh):
                u = i * kh + h
                packed[k - 1][u * width : (u + 1) * width, :] = n_all[k * per + i, h].astype(jnp.bfloat16)
                pieces = split_three(m_all[k * per + i, h]) + split_three(l_all[k * per + i, h])
                for c, piece in enumerate(pieces):
                    stats = jnp.where(lane == 6 * u + c, piece, stats)
        u = per * kh
        packed[k - 1][u * width : (u + 1) * width, :] = stats.astype(jnp.bfloat16)


def prefix_attention(prompt_of, queries, keys, keys_got, values, values_got, own, scale):
    roll = len(queries)
    per, kh, width, _ = queries[0].shape
    prompts, span, _ = keys.shape
    vmem = pl.BlockSpec(memory_space=pltpu.VMEM)
    rows = (per * kh + 1) * width
    out = jax.ShapeDtypeStruct(queries[0].shape, jnp.float32)
    elements = roll * per * kh * width * span * 2
    everything = (roll * per, kh, width, HD)
    outs = pl.pallas_call(
        functools.partial(prefix_kernel, scale, roll),
        in_specs=[pl.BlockSpec(memory_space=pltpu.SMEM)] + [vmem] * (roll + 7),
        out_specs=[vmem] * (roll + 2),
        scratch_shapes=[pltpu.VMEM(everything, jnp.bfloat16)]
        + [pltpu.VMEM(everything, jnp.float32)] * 3
        + [pltpu.SMEM((roll * per,), jnp.int32)],
        out_shape=[out] * 3 + [jax.ShapeDtypeStruct((rows, HD), jnp.bfloat16)] * (roll - 1),
        compiler_params=pltpu.CompilerParams(vmem_limit_bytes=12 << 20),
        cost_estimate=pl.CostEstimate(
            flops=4 * elements * HD, bytes_accessed=8 * prompts * span * kh * HD, transcendentals=elements
        ),
        name="prefix_attention",
    )(prompt_of, *queries, keys, keys_got, values, values_got, *own)
    return outs[:3], outs[3:]


def merge_kernel(group, n_ref, m_ref, l_ref, *refs):
    packed, out_ref = refs[:-1], refs[-1]
    per, kh, width, _ = n_ref.shape
    guess = width // group
    stats = [p[per * kh * width :, :].astype(jnp.float32) for p in packed]
    results = {}
    for i in range(per):
        for h in range(kh):
            u = i * kh + h

            def column(s, c):
                c = 6 * u + c
                return s[:, c : c + 1] + s[:, c + 1 : c + 2] + s[:, c + 2 : c + 3]

            peaks = [m_ref[i, h]] + [jnp.broadcast_to(column(s, 0), (width, HD)) for s in stats]
            totals = [l_ref[i, h]] + [jnp.broadcast_to(column(s, 3), (width, HD)) for s in stats]
            numers = [n_ref[i, h]] + [p[u * width : (u + 1) * width, :].astype(jnp.float32) for p in packed]
            top = functools.reduce(jnp.maximum, peaks)
            total = jnp.zeros((width, HD), jnp.float32)
            numer = jnp.zeros((width, HD), jnp.float32)
            for m, l, n in zip(peaks, totals, numers):
                f = jnp.exp(m - top)
                total = total + l * f
                numer = numer + n * f
            results[i, h] = numer / total
    for h in range(kh):
        for g in range(group):
            rows = [results[i, h][g * guess : (g + 1) * guess] for i in range(per)]
            at = (h * group + g) * HD
            out_ref[:, at : at + HD] = jnp.concatenate(rows, axis=0).astype(jnp.bfloat16)


def merge(own, packed, group):
    per, kh, width, _ = own[0].shape
    whole = pl.BlockSpec(own[0].shape, lambda n: (0, 0, 0, 0))
    sent = pl.BlockSpec(packed[0].shape, lambda n: (0, 0))
    shape = (per * width // group, kh * group * HD)
    return pl.pallas_call(
        functools.partial(merge_kernel, group),
        grid=(1,),
        out_shape=jax.ShapeDtypeStruct(shape, jnp.bfloat16),
        in_specs=[whole] * 3 + [sent] * len(packed),
        out_specs=pl.BlockSpec(shape, lambda n: (0, 0)),
        compiler_params=pltpu.CompilerParams(vmem_limit_bytes=16 << 20),
        name="merge",
    )(*own, *packed)


def output_kernel(roll, theirs, *refs):
    parts, w_ref, rest = refs[:roll], refs[roll], refs[roll + 1 :]
    lhs = rest[-1]
    zone, seq, tp = lax.axis_index("roll"), lax.axis_index("seq"), lax.axis_index("tp")
    block, cols = parts[0].shape
    side = 1 - seq if theirs else seq
    for k in range(roll):
        at = pl.multiple_of((zone ^ k ^ (tp * (roll // 2))) * block, block)
        lhs[pl.ds(at, block), :] = parts[k][...]
    w = w_ref[pl.ds(pl.multiple_of(side * cols, cols), cols), :]
    part = jnp.dot(lhs[...], w, preferred_element_type=jnp.float32)
    if not theirs:
        rest[0][...] = part
        return
    part = rest[0][...] + part
    keep_ref, send_ref = rest[1:3]
    rows = keep_ref.shape[0]
    keep_ref[...] = part[:rows]
    send_ref[...] = part[rows:].astype(send_ref.dtype)


def output(parts, w_out, before=None):
    roll = len(parts)
    block, cols = parts[0].shape
    width = w_out.shape[1]
    rows = roll * block
    vmem = pl.BlockSpec(memory_space=pltpu.VMEM)
    theirs = before is not None
    if theirs:
        shapes = [
            jax.ShapeDtypeStruct((rows // 2, width), jnp.float32),
            jax.ShapeDtypeStruct((rows // 2, width), jnp.bfloat16),
        ]
    else:
        shapes = jax.ShapeDtypeStruct((rows, width), jnp.float32)
    return pl.pallas_call(
        functools.partial(output_kernel, roll, theirs),
        in_specs=[vmem] * (roll + 1 + theirs),
        out_specs=[vmem, vmem] if theirs else vmem,
        scratch_shapes=[pltpu.VMEM((rows, cols), jnp.bfloat16)],
        out_shape=shapes,
        compiler_params=pltpu.CompilerParams(vmem_limit_bytes=16 << 20),
        cost_estimate=pl.CostEstimate(
            flops=2 * rows * cols * width, bytes_accessed=2 * cols * width, transcendentals=0
        ),
        name="output_theirs" if theirs else "output_mine",
    )(*parts, w_out, *((before,) if theirs else ()))


def fast_body(
    hidden,
    w_query,
    w_key,
    w_value,
    b_query,
    b_key,
    b_value,
    w_out,
    prefix_keys,
    prefix_values,
    suffix_keys,
    suffix_values,
    suffix_lengths,
    prompt_of,
):
    roll = lax.axis_size("roll")
    kv_heads = w_key.shape[1] // HD
    group = w_query.shape[1] // w_key.shape[1]
    kh = kv_heads // 2
    per = suffix_keys.shape[0]
    block = hidden.shape[0] // roll
    guess = block // per
    scale = 1.0 / math.sqrt(HD)

    def across(x):
        return lax.ppermute(x, "seq", [(0, 1), (1, 0)])

    def hop(x, k):
        return lax.ppermute(x, "roll", [(n, n ^ k) for n in range(roll)])

    def hops(pick):
        sent = {k: hop(pick(k), k) for k in reversed(range(1, roll))}
        return [sent[k] for k in range(1, roll)]

    send, keep = project(hidden, w_query, w_key, w_value, roll, kh)
    got = across(send)
    terms = [keep[k] + got[k] for k in range(roll)]
    if roll == 4:
        relayed = hop(terms[3], 1)
        near = hop(terms[1], 1)
        sums = [terms[0], near, hop(terms[2] + relayed, 2)]
    else:
        sums = [terms[0]] + hops(lambda k: terms[k])
    caches = (suffix_keys, suffix_values, prefix_keys, prefix_values)
    _, small = lax.optimization_barrier(
        (terms[0], (suffix_lengths, b_query, b_key, b_value, *caches))
    )
    caches = small[4:]

    sk_got, sv_got, pk_got, pv_got = [across(x) for x in caches]
    sk_own, sv_own, pk_own, pv_own = fetch(caches)

    row_ids = jnp.arange(hidden.shape[0], dtype=jnp.int32)
    prefix_total = prefix_keys.shape[1] * roll * 2
    positions = (prefix_total + lookup(small[0], row_ids // guess) + row_ids % guess).astype(jnp.float32)
    half = HD // 2
    steps = jnp.arange(half).astype(jnp.float32) * (2.0 / HD)
    freqs = jnp.exp(-math.log(ROPE_BASE) * steps)
    angles = positions[:, None] * freqs[None, :]
    cosine = jnp.cos(angles)
    sine = jnp.sin(angles)
    cosine = jnp.concatenate([cosine, cosine], axis=-1)
    sine = jnp.concatenate([-sine, sine], axis=-1)
    biases = [b[None, :] for b in small[1:4]]

    q, k_new, v_new = finish(sums, biases, cosine, sine, per)
    queries = [q] + hops(lambda k: q)
    own = own_attention(
        suffix_lengths, q, k_new, v_new, sk_own, sk_got, sv_own, sv_got, scale, guess
    )
    own, packed = prefix_attention(
        prompt_of, queries, pk_own, pk_got, pv_own, pv_got, own, scale
    )
    packed = hops(lambda k: packed[k - 1])
    share = merge(own, packed, group)
    mine = [share] + hops(lambda k: share)
    theirs = [across(m) for m in mine]
    kept, sent = output(theirs, w_out, output(mine, w_out))
    arrived = lax.ppermute(sent, "tp", [(0, 1), (1, 0)])
    return (kept + arrived.astype(jnp.float32)).astype(jnp.bfloat16)


def body(*arrays):
    hidden, w_key, prompt_of, suffix_keys = arrays[0], arrays[2], arrays[13], arrays[10]
    roll = lax.axis_size("roll")
    block = hidden.shape[0] // roll
    fits = (
        lax.axis_size("seq") == 2
        and lax.axis_size("tp") == 2
        and roll & (roll - 1) == 0
        and (w_key.shape[1] // HD) % 2 == 0
        and block % 16 == 0
        and block == suffix_keys.shape[0] * GUESS
        and 6 * suffix_keys.shape[0] * (w_key.shape[1] // HD) <= 2 * HD
        and prompt_of.shape[0] % arrays[8].shape[0] == 0
    )
    if not fits:
        return general_body(*arrays)
    return fast_body(*arrays)


def solution(mesh):
    return jax.shard_map(
        body,
        mesh=mesh,
        in_specs=(
            P("groups", ("roll", "seq")),
            P(("roll", "seq"), "tp"),
            P(("roll", "seq"), "tp"),
            P(("roll", "seq"), "tp"),
            P("tp"),
            P("tp"),
            P("tp"),
            P("tp", ("roll", "seq")),
            P("groups", ("roll", "seq"), "tp"),
            P("groups", ("roll", "seq"), "tp"),
            P(("groups", "roll"), "seq", "tp"),
            P(("groups", "roll"), "seq", "tp"),
            P("groups"),
            P("groups"),
        ),
        out_specs=P(("groups", "tp"), ("roll", "seq")),
        check_vma=False,
    )
```

```python
import functools
import math

import jax
import jax.numpy as jnp
from jax import lax
from jax.experimental import pallas as pl
from jax.experimental.pallas import tpu as pltpu
from jax.sharding import PartitionSpec as P


HD = 128
GUESS = 8


ROPE_BASE = 1000000.0
NEG_FILL = -1e30


def rotate(values, positions):
    half = values.shape[-1] // 2
    steps = jnp.arange(half).astype(jnp.float32) * (2.0 / values.shape[-1])
    freqs = jnp.exp(-math.log(ROPE_BASE) * steps)
    angles = positions[:, None] * freqs[None, :]
    cosine = jnp.cos(angles)[:, None, :]
    sine = jnp.sin(angles)[:, None, :]
    first = values[..., :half]
    second = values[..., half:]
    return jnp.concatenate(
        [first * cosine - second * sine, second * cosine + first * sine], axis=-1
    )


def lookup(table, indices):
    hits = indices[:, None] == jnp.arange(table.shape[0], dtype=jnp.int32)[None, :]
    return jnp.sum(jnp.where(hits, table[None, :], 0), axis=1)


def combine(first, second):
    peak_a, total_a, numer_a = first
    peak_b, total_b, numer_b = second
    peak = jnp.maximum(peak_a, peak_b)
    factor_a = jnp.exp(peak_a - peak)
    factor_b = jnp.exp(peak_b - peak)
    return (
        peak,
        total_a * factor_a + total_b * factor_b,
        numer_a * factor_a[..., None] + numer_b * factor_b[..., None],
    )


def masked_stats(scores, visible, values):
    peak = jnp.max(jnp.where(visible, scores, NEG_FILL), axis=-1)
    weights = jnp.exp(jnp.where(visible, scores - peak[..., None], NEG_FILL))
    total = jnp.sum(weights, axis=-1)
    numer = jnp.einsum(
        "rtkgs,rskd->rtkgd",
        weights.astype(jnp.bfloat16),
        values,
        preferred_element_type=jnp.float32,
    )
    return (peak, total, numer)


def general_body(
    hidden,
    w_query,
    w_key,
    w_value,
    b_query,
    b_key,
    b_value,
    w_out,
    prefix_keys,
    prefix_values,
    suffix_keys,
    suffix_values,
    suffix_lengths,
    prompt_of,
):
    row_count = hidden.shape[0]
    q_heads = w_query.shape[1] // HD
    kv_heads = w_key.shape[1] // HD
    group = q_heads // kv_heads
    prompts = prefix_keys.shape[0]
    pre_dev = prefix_keys.shape[1]
    prefix_total = pre_dev * lax.axis_size(("roll", "seq"))
    per_device = suffix_keys.shape[0]
    suf_dev = suffix_keys.shape[1]
    scale = 1.0 / math.sqrt(HD)
    q_part = jnp.dot(hidden, w_query, preferred_element_type=jnp.float32)
    k_part = jnp.dot(hidden, w_key, preferred_element_type=jnp.float32)
    v_part = jnp.dot(hidden, w_value, preferred_element_type=jnp.float32)
    q_sum, k_sum, v_sum = lax.psum((q_part, k_part, v_part), ("roll", "seq"))
    count = q_sum.shape[0]
    row_ids = jnp.arange(count, dtype=jnp.int32)
    owner_ids = row_ids // GUESS
    positions = (prefix_total + lookup(suffix_lengths, owner_ids) + row_ids % GUESS).astype(
        jnp.float32
    )
    q_rot = rotate((q_sum + b_query.astype(jnp.float32)).reshape(count, q_heads, HD), positions)
    k_rot = rotate((k_sum + b_key.astype(jnp.float32)).reshape(count, kv_heads, HD), positions)
    v_fin = (v_sum + b_value.astype(jnp.float32)).reshape(count, kv_heads, HD)
    query = q_rot.astype(jnp.bfloat16)
    key_new = k_rot.astype(jnp.bfloat16)
    value_new = v_fin.astype(jnp.bfloat16)
    query_grid = query.reshape(row_count, kv_heads, group, HD)
    owners_all = jnp.arange(row_count, dtype=jnp.int32) // GUESS
    row_prompt = lookup(prompt_of, owners_all)
    pre_keys = prefix_keys.reshape(prompts, pre_dev, kv_heads, HD)
    pre_values = prefix_values.reshape(prompts, pre_dev, kv_heads, HD)
    peak_all = jnp.full((row_count, kv_heads, group), NEG_FILL, jnp.float32)
    total_all = jnp.zeros((row_count, kv_heads, group), jnp.float32)
    numer_all = jnp.zeros((row_count, kv_heads, group, HD), jnp.float32)
    for prompt in range(prompts):
        scores = (
            jnp.einsum(
                "tkgd,skd->tkgs", query_grid, pre_keys[prompt], preferred_element_type=jnp.float32
            )
            * scale
        )
        block_peak = jnp.max(scores, axis=-1)
        weights = jnp.exp(scores - block_peak[..., None])
        block_numer = jnp.einsum(
            "tkgs,skd->tkgd",
            weights.astype(jnp.bfloat16),
            pre_values[prompt],
            preferred_element_type=jnp.float32,
        )
        picked = (row_prompt == prompt)[:, None, None]
        peak_all = jnp.where(picked, block_peak, peak_all)
        total_all = jnp.where(picked, jnp.sum(weights, axis=-1), total_all)
        numer_all = jnp.where(picked[..., None], block_numer, numer_all)
    first_rollout = lax.axis_index("roll") * per_device
    seq_index = lax.axis_index("seq")
    local_len = lax.dynamic_slice_in_dim(suffix_lengths, first_rollout, per_device, 0)
    live = jnp.clip(local_len - seq_index * suf_dev, 0, suf_dev)
    row_start = first_rollout * GUESS
    local_rows = per_device * GUESS
    query_local = lax.dynamic_slice_in_dim(query_grid, row_start, local_rows, 0).reshape(
        per_device, GUESS, kv_heads, group, HD
    )
    suf_keys = suffix_keys.reshape(per_device, suf_dev, kv_heads, HD)
    suf_values = suffix_values.reshape(per_device, suf_dev, kv_heads, HD)
    scores = (
        jnp.einsum("rtkgd,rskd->rtkgs", query_local, suf_keys, preferred_element_type=jnp.float32)
        * scale
    )
    visible = (jnp.arange(suf_dev, dtype=jnp.int32)[None, :] < live[:, None])[
        :, None, None, None, :
    ]
    suffix_part = masked_stats(scores, visible, suf_values)
    key_local = lax.dynamic_slice_in_dim(key_new, row_start, local_rows, 0).reshape(
        per_device, GUESS, kv_heads, HD
    )
    value_local = lax.dynamic_slice_in_dim(value_new, row_start, local_rows, 0).reshape(
        per_device, GUESS, kv_heads, HD
    )
    new_scores = (
        jnp.einsum("rtkgd,rskd->rtkgs", query_local, key_local, preferred_element_type=jnp.float32)
        * scale
    )
    guess_ids = jnp.arange(GUESS, dtype=jnp.int32)
    causal = (guess_ids[None, :] <= guess_ids[:, None]) & (seq_index == 0)
    guess_part = masked_stats(new_scores, causal[None, :, None, None, :], value_local)
    prefix_local = (
        lax.dynamic_slice_in_dim(peak_all, row_start, local_rows, 0).reshape(
            per_device, GUESS, kv_heads, group
        ),
        lax.dynamic_slice_in_dim(total_all, row_start, local_rows, 0).reshape(
            per_device, GUESS, kv_heads, group
        ),
        lax.dynamic_slice_in_dim(numer_all, row_start, local_rows, 0).reshape(
            per_device, GUESS, kv_heads, group, HD
        ),
    )
    peak_loc, total_loc, numer_loc = combine(combine(prefix_local, suffix_part), guess_part)
    peak_all = lax.dynamic_update_slice_in_dim(
        peak_all, peak_loc.reshape(local_rows, kv_heads, group), row_start, 0
    )
    total_all = lax.dynamic_update_slice_in_dim(
        total_all, total_loc.reshape(local_rows, kv_heads, group), row_start, 0
    )
    numer_all = lax.dynamic_update_slice_in_dim(
        numer_all, numer_loc.reshape(local_rows, kv_heads, group, HD), row_start, 0
    )
    peaks, totals, numers = (
        lax.all_to_all(peak_all[None], ("roll", "seq"), split_axis=1, concat_axis=0, tiled=True),
        lax.all_to_all(total_all[None], ("roll", "seq"), split_axis=1, concat_axis=0, tiled=True),
        lax.all_to_all(numer_all[None], ("roll", "seq"), split_axis=1, concat_axis=0, tiled=True),
    )
    peak_top = jnp.max(peaks, axis=0)
    factors = jnp.exp(peaks - peak_top[None])
    share = (
        jnp.sum(numers * factors[..., None], axis=0) / jnp.sum(totals * factors, axis=0)[..., None]
    )
    share = share.astype(jnp.bfloat16).reshape(share.shape[0], q_heads * HD)
    attention = lax.all_gather(share, ("roll", "seq"), axis=0, tiled=True)
    summed = lax.psum_scatter(
        jnp.dot(attention, w_out, preferred_element_type=jnp.float32),
        "tp",
        scatter_dimension=0,
        tiled=True,
    )
    return summed.astype(jnp.bfloat16)


SEND_LIMIT = 12 << 20
STATS = 16
LOG2E = 1.4426950408889634


def contract_last(a, b):
    return lax.dot_general(a, b, (((1,), (1,)), ((), ())), preferred_element_type=jnp.float32)


def place(out_ref, part, at, block):
    zone = lax.axis_index("roll")
    roll, _, _, width = out_ref.shape
    j, at = at // width, at % width
    for b in range(roll):
        out_ref[b ^ zone, j, :, at : at + part.shape[1]] = part[b * block : (b + 1) * block]


def place_all(x, weights, out_ref, ready):
    *wq, wk, wv = weights
    _, kh, block, width = out_ref.shape
    chunks = len(wq)
    span = wq[0].shape[1]
    wide = width - 2 * HD
    for c, w, at in ((chunks, wk, wide), (chunks + 1, wv, wide + HD)):
        ready(c)
        part = jnp.dot(x, w[...], preferred_element_type=jnp.float32)
        for j in range(kh):
            place(out_ref, part[:, j * HD : (j + 1) * HD], j * width + at, block)
    for c in range(chunks):
        ready(c)
        part = jnp.dot(x, wq[c][...], preferred_element_type=jnp.float32)
        place(out_ref, part, c * span // wide * width + c * span % wide, block)


def project_kernel(x_ref, wq_ref, wk_ref, wv_ref, send_ref, keep_ref, x_all, *refs):
    seq = lax.axis_index("seq")
    sems = refs[-1]
    count = len(refs) // 2
    sources = [wq_ref] * (count - 2) + [wk_ref, wv_ref]

    def copies(half, targets, at):
        made = []
        for n, (source, target) in enumerate(zip(sources, targets)):
            span = target.shape[1]
            start = half * (source.shape[1] // 2) + (n * span if n < count - 2 else 0)
            part = source.at[:, pl.ds(pl.multiple_of(start, span), span)]
            made.append(pltpu.make_async_copy(part, target, sems.at[at + n]))
        return made

    fetch = pltpu.make_async_copy(x_ref, x_all, sems.at[2 * count])
    fetch.start()
    work = []
    for half, out_ref, at in ((1 - seq, send_ref, 0), (seq, keep_ref, count)):
        targets = refs[at : at + count]
        started = copies(half, targets, at)
        for copy in started[-2:] + started[:-2]:
            copy.start()
        work.append((targets, out_ref, started))
    fetch.wait()
    for targets, out_ref, started in work:
        place_all(x_all[...], targets, out_ref, lambda c: started[c].wait())


def project(hidden, w_query, w_key, w_value, roll, kh):
    rows, depth = hidden.shape
    kv_heads = w_key.shape[1] // HD
    wide = w_query.shape[1] // kv_heads
    block = rows // roll
    width = wide + 2 * HD
    span = min(wide, 512)
    chunks = kh * wide // span
    hbm = pl.BlockSpec(memory_space=pltpu.HBM)
    vmem = pl.BlockSpec(memory_space=pltpu.VMEM)
    shapes = ([(depth, span)] * chunks + [(depth, kh * HD)] * 2) * 2
    out = jax.ShapeDtypeStruct((roll, kh, block, width), jnp.float32)
    return pl.pallas_call(
        project_kernel,
        out_shape=[out, out],
        in_specs=[hbm] * 4,
        out_specs=[vmem, vmem],
        scratch_shapes=[pltpu.VMEM((rows, depth), jnp.bfloat16)]
        + [pltpu.VMEM(s, jnp.bfloat16) for s in shapes]
        + [pltpu.SemaphoreType.DMA((len(shapes) + 1,))],
        compiler_params=pltpu.CompilerParams(vmem_limit_bytes=SEND_LIMIT),
        cost_estimate=pl.CostEstimate(
            flops=4 * rows * depth * width * kh, bytes_accessed=4 * depth * width * kh, transcendentals=0
        ),
        name="project",
    )(*[pltpu.with_memory_space_constraint(a, pltpu.HBM) for a in (hidden, w_query, w_key, w_value)])


def finish_kernel(group, per, kh, *refs):
    bq_ref, bk_ref, bv_ref, cos_ref, sin_ref, q_ref, k_ref, v_ref = refs[-8:]
    sums = refs[:-8]
    block = sums[0].shape[1]
    guess = block // per
    seq = lax.axis_index("seq")
    rows = pl.ds(pl.multiple_of(lax.axis_index("roll") * block, block), block)
    cosine = cos_ref[rows, :]
    sine = sin_ref[rows, :]

    def bias_of(ref, n):
        at = seq * (ref.shape[1] // 2) + n * HD
        return ref[:, pl.ds(pl.multiple_of(at, HD), HD)]

    def total(j, g):
        at = slice(g * HD, (g + 1) * HD)
        u = sums[0][j, :, at]
        for o in sums[1:]:
            u = u + o[j, :, at]
        if g < group:
            bias = bias_of(bq_ref, j * group + g)
        else:
            bias = bias_of(bk_ref if g == group else bv_ref, j)
        return u + bias.astype(jnp.float32)

    def turn(u):
        return u * cosine + pltpu.roll(u, HD // 2, 1) * sine

    for j in range(kh):
        for g in range(0, group, 2):
            one = turn(total(j, g))
            two = turn(total(j, g + 1))
            for i in range(per):
                span = slice(i * guess, (i + 1) * guess)
                both = jnp.concatenate([one[span], two[span]], axis=0)
                q_ref[i, j, g * guess : (g + 2) * guess, :] = both.astype(jnp.bfloat16)
        k_ref[j] = turn(total(j, group)).astype(jnp.bfloat16)
        v_ref[j] = total(j, group + 1).astype(jnp.bfloat16)


def finish(sums, biases, cosine, sine, per):
    kh, block, width = sums[0].shape
    group = width // HD - 2
    guess = block // per
    vmem = pl.BlockSpec(memory_space=pltpu.VMEM)
    return pl.pallas_call(
        functools.partial(finish_kernel, group, per, kh),
        in_specs=[vmem] * (len(sums) + len(biases) + 2),
        out_specs=[vmem] * 3,
        out_shape=(
            jax.ShapeDtypeStruct((per, kh, group * guess, HD), jnp.bfloat16),
            jax.ShapeDtypeStruct((kh, block, HD), jnp.bfloat16),
            jax.ShapeDtypeStruct((kh, block, HD), jnp.bfloat16),
        ),
        compiler_params=pltpu.CompilerParams(vmem_limit_bytes=16 << 20),
        name="finish",
    )(*sums, *biases, cosine, sine)


def fetch_kernel(*refs):
    count = len(refs) // 2
    sems = refs[-1]
    seq = lax.axis_index("seq")
    copies = []
    for n, (source, target) in enumerate(zip(refs[:count], refs[count:-1])):
        cols = target.shape[2]
        part = source.at[:, :, pl.ds(pl.multiple_of(seq * cols, cols), cols)]
        copies.append(pltpu.make_async_copy(part, target, sems.at[n]))
    for copy in copies:
        copy.start()
    for copy in copies:
        copy.wait()


def fetch(caches):
    shapes = [(c.shape[0], c.shape[1], c.shape[2] // 2) for c in caches]
    return pl.pallas_call(
        fetch_kernel,
        in_specs=[pl.BlockSpec(memory_space=pltpu.HBM)] * len(caches),
        out_specs=[pl.BlockSpec(memory_space=pltpu.VMEM)] * len(caches),
        out_shape=[jax.ShapeDtypeStruct(s, jnp.bfloat16) for s in shapes],
        scratch_shapes=[pltpu.SemaphoreType.DMA((len(caches),))],
        compiler_params=pltpu.CompilerParams(vmem_limit_bytes=1 << 20),
        cost_estimate=pl.CostEstimate(
            flops=0, bytes_accessed=2 * sum(math.prod(s) for s in shapes), transcendentals=0
        ),
        name="fetch",
    )(*[pltpu.with_memory_space_constraint(c, pltpu.HBM) for c in caches])


def own_kernel(scale, guess, lengths, q_ref, kn_ref, vn_ref, k0_ref, k1_ref, v0_ref, v1_ref, n_ref, m_ref, l_ref):
    per, kh, width, _ = q_ref.shape
    span = k0_ref.shape[1]
    seq = lax.axis_index("seq")
    zone = lax.axis_index("roll")
    fresh = kn_ref.shape[1]
    key_id = lax.broadcasted_iota(jnp.int32, (width, span), 1)
    new_id = lax.broadcasted_iota(jnp.int32, (width, fresh), 1)
    row_id = lax.broadcasted_iota(jnp.int32, (width, fresh), 0) % guess
    for i in range(per):
        length = lengths[zone * per + i]
        sees = (key_id < length - seq * span, key_id < length - (1 - seq) * span)
        causal = (new_id >= i * guess) & (new_id - i * guess <= row_id)
        sees = sees + (causal,)
        for j in range(kh):
            q = q_ref[i, j]
            at = pl.ds(pl.multiple_of((seq * kh + j) * HD, HD), HD)
            mine = slice(j * HD, (j + 1) * HD)
            keys = (k0_ref[i, :, mine], k1_ref[i, :, at], kn_ref[j])
            values = (v0_ref[i, :, mine], v1_ref[i, :, at], vn_ref[j])
            scores = [jnp.where(see, contract_last(q, k), NEG_FILL) for k, see in zip(keys, sees)]
            peak = jnp.max(scores[0], axis=1, keepdims=True)
            for s in scores[1:]:
                peak = jnp.maximum(peak, jnp.max(s, axis=1, keepdims=True))
            total = jnp.zeros((width, 1), jnp.float32)
            numer = jnp.zeros((width, HD), jnp.float32)
            for s, v in zip(scores, values):
                w = jnp.exp2((s - peak) * (scale * LOG2E))
                total = total + jnp.sum(w, axis=1, keepdims=True)
                numer = numer + jnp.dot(w.astype(jnp.bfloat16), v, preferred_element_type=jnp.float32)
            peak = peak * scale
            n_ref[i, j] = numer
            m_ref[i, j] = jnp.broadcast_to(peak, (width, HD))
            l_ref[i, j] = jnp.broadcast_to(total, (width, HD))


def own_attention(lengths, q, k_new, v_new, keys, keys_got, values, values_got, scale, guess):
    per, kh, width, _ = q.shape
    span = keys.shape[1]
    vmem = pl.BlockSpec(memory_space=pltpu.VMEM)
    out = jax.ShapeDtypeStruct(q.shape, jnp.float32)
    elements = per * kh * width * span * 2
    return pl.pallas_call(
        functools.partial(own_kernel, scale, guess),
        in_specs=[pl.BlockSpec(memory_space=pltpu.SMEM)] + [vmem] * 7,
        out_specs=[vmem] * 3,
        out_shape=(out, out, out),
        compiler_params=pltpu.CompilerParams(vmem_limit_bytes=12 << 20),
        cost_estimate=pl.CostEstimate(
            flops=4 * elements * HD, bytes_accessed=8 * per * span * kh * HD, transcendentals=elements
        ),
        name="own_attention",
    )(lengths, q, k_new, v_new, keys, keys_got, values, values_got)


def split_three(x):
    high = x.astype(jnp.bfloat16).astype(jnp.float32)
    rest = x - high
    middle = rest.astype(jnp.bfloat16).astype(jnp.float32)
    return high, middle, rest - middle


def prefix_kernel(scale, roll, prompts, *refs):
    q_refs = refs[:roll]
    k0_ref, k1_ref, v0_ref, v1_ref, on_ref, om_ref, ol_ref = refs[roll : roll + 7]
    n_out, m_out, l_out = refs[roll + 7 : roll + 10]
    packed = refs[roll + 10 : 2 * roll + 9]
    q_all, n_all, m_all, l_all, order = refs[2 * roll + 9 :]
    per, kh, width, _ = q_refs[0].shape
    zone = lax.axis_index("roll")
    seq = lax.axis_index("seq")
    count = k0_ref.shape[0]
    share = roll * per // count

    for k in range(roll):
        q_all[k * per : (k + 1) * per] = q_refs[k][...]
    filled = [jnp.int32(p * share) for p in range(count)]
    for k in range(roll):
        for i in range(per):
            owner = prompts[(zone ^ k) * per + i]
            for p in range(count):
                chosen = owner == p

                @pl.when(chosen)
                def _():
                    order[filled[p]] = k * per + i

                filled[p] = filled[p] + chosen.astype(jnp.int32)

    for p in range(count):
        ids = [order[p * share + n] for n in range(share)]
        for j in range(kh):
            at = pl.ds(pl.multiple_of((seq * kh + j) * HD, HD), HD)
            q = jnp.concatenate([q_all[n, j] for n in ids], axis=0)
            mine = slice(j * HD, (j + 1) * HD)
            scores = [contract_last(q, k_ref[p, :, to]) for k_ref, to in ((k0_ref, mine), (k1_ref, at))]
            peak = jnp.maximum(
                jnp.max(scores[0], axis=1, keepdims=True), jnp.max(scores[1], axis=1, keepdims=True)
            )
            total = jnp.zeros(peak.shape, jnp.float32)
            numer = jnp.zeros((share * width, HD), jnp.float32)
            for s, v_ref, to in zip(scores, (v0_ref, v1_ref), (mine, at)):
                w = jnp.exp2((s - peak) * (scale * LOG2E))
                total = total + jnp.sum(w, axis=1, keepdims=True)
                numer = numer + jnp.dot(
                    w.astype(jnp.bfloat16), v_ref[p, :, to], preferred_element_type=jnp.float32
                )
            peak = jnp.broadcast_to(peak * scale, numer.shape)
            total = jnp.broadcast_to(total, numer.shape)
            for n, slot in enumerate(ids):
                span = slice(n * width, (n + 1) * width)
                n_all[slot, j] = numer[span]
                m_all[slot, j] = peak[span]
                l_all[slot, j] = total[span]

    for i in range(per):
        for h in range(kh):
            m_a, m_b = m_all[i, h], om_ref[i, h]
            peak = jnp.maximum(m_a, m_b)
            f_a, f_b = jnp.exp(m_a - peak), jnp.exp(m_b - peak)
            m_out[i, h] = peak
            l_out[i, h] = l_all[i, h] * f_a + ol_ref[i, h] * f_b
            n_out[i, h] = n_all[i, h] * f_a + on_ref[i, h] * f_b
    lane = lax.broadcasted_iota(jnp.int32, (width, HD), 1)
    for k in range(1, roll):
        peaks = jnp.zeros((width, HD), jnp.float32)
        totals = jnp.zeros((width, HD), jnp.float32)
        for i in range(per):
            for h in range(kh):
                u = i * kh + h
                at = k * per + i
                packed[k - 1][u * width : (u + 1) * width, :] = n_all[at, h].astype(jnp.bfloat16)
                for c, (m, l) in enumerate(zip(split_three(m_all[at, h]), split_three(l_all[at, h]))):
                    peaks = jnp.where(lane == 3 * u + c, m, peaks)
                    totals = jnp.where(lane == 3 * u + c, l, totals)
        stats = jnp.concatenate([peaks, totals], axis=0).T
        packed[k - 1][per * kh * width :, :] = stats[:STATS].astype(jnp.bfloat16)


def prefix_attention(prompt_of, queries, keys, keys_got, values, values_got, own, scale):
    roll = len(queries)
    per, kh, width, _ = queries[0].shape
    prompts, span, _ = keys.shape
    vmem = pl.BlockSpec(memory_space=pltpu.VMEM)
    rows = per * kh * width + STATS
    out = jax.ShapeDtypeStruct(queries[0].shape, jnp.float32)
    elements = roll * per * kh * width * span * 2
    everything = (roll * per, kh, width, HD)
    outs = pl.pallas_call(
        functools.partial(prefix_kernel, scale, roll),
        in_specs=[pl.BlockSpec(memory_space=pltpu.SMEM)] + [vmem] * (roll + 7),
        out_specs=[vmem] * (roll + 2),
        scratch_shapes=[pltpu.VMEM(everything, jnp.bfloat16)]
        + [pltpu.VMEM(everything, jnp.float32)] * 3
        + [pltpu.SMEM((roll * per,), jnp.int32)],
        out_shape=[out] * 3 + [jax.ShapeDtypeStruct((rows, HD), jnp.bfloat16)] * (roll - 1),
        compiler_params=pltpu.CompilerParams(vmem_limit_bytes=12 << 20),
        cost_estimate=pl.CostEstimate(
            flops=4 * elements * HD, bytes_accessed=8 * prompts * span * kh * HD, transcendentals=elements
        ),
        name="prefix_attention",
    )(prompt_of, *queries, keys, keys_got, values, values_got, *own)
    return outs[:3], outs[3:]


def merge_kernel(group, n_ref, m_ref, l_ref, *refs):
    packed, out_ref = refs[:-1], refs[-1]
    per, kh, width, _ = n_ref.shape
    guess = width // group
    blank = jnp.zeros((HD - STATS, HD), jnp.float32)
    stats = [
        jnp.concatenate([p[per * kh * width :, :].astype(jnp.float32), blank], axis=0).T for p in packed
    ]
    results = {}
    for i in range(per):
        for h in range(kh):
            u = i * kh + h

            def column(s, n):
                s = s[n * width : (n + 1) * width]
                c = 3 * u
                return s[:, c : c + 1] + s[:, c + 1 : c + 2] + s[:, c + 2 : c + 3]

            peaks = [m_ref[i, h]] + [jnp.broadcast_to(column(s, 0), (width, HD)) for s in stats]
            totals = [l_ref[i, h]] + [jnp.broadcast_to(column(s, 1), (width, HD)) for s in stats]
            numers = [n_ref[i, h]] + [p[u * width : (u + 1) * width, :].astype(jnp.float32) for p in packed]
            top = functools.reduce(jnp.maximum, peaks)
            total = jnp.zeros((width, HD), jnp.float32)
            numer = jnp.zeros((width, HD), jnp.float32)
            for m, l, n in zip(peaks, totals, numers):
                f = jnp.exp(m - top)
                total = total + l * f
                numer = numer + n * f
            results[i, h] = numer / total
    for h in range(kh):
        for g in range(group):
            rows = [results[i, h][g * guess : (g + 1) * guess] for i in range(per)]
            at = (h * group + g) * HD
            out_ref[:, at : at + HD] = jnp.concatenate(rows, axis=0).astype(jnp.bfloat16)


def merge(own, packed, group):
    per, kh, width, _ = own[0].shape
    whole = pl.BlockSpec(own[0].shape, lambda n: (0, 0, 0, 0))
    sent = pl.BlockSpec(packed[0].shape, lambda n: (0, 0))
    shape = (per * width // group, kh * group * HD)
    return pl.pallas_call(
        functools.partial(merge_kernel, group),
        grid=(1,),
        out_shape=jax.ShapeDtypeStruct(shape, jnp.bfloat16),
        in_specs=[whole] * 3 + [sent] * len(packed),
        out_specs=pl.BlockSpec(shape, lambda n: (0, 0)),
        compiler_params=pltpu.CompilerParams(vmem_limit_bytes=16 << 20),
        name="merge",
    )(*own, *packed)


def output_kernel(roll, theirs, *refs):
    parts, w_ref, rest = refs[:roll], refs[roll], refs[roll + 1 :]
    lhs = rest[-1]
    zone, seq, tp = lax.axis_index("roll"), lax.axis_index("seq"), lax.axis_index("tp")
    block, cols = parts[0].shape
    side = 1 - seq if theirs else seq
    for k in range(roll):
        at = pl.multiple_of((zone ^ k ^ (tp * (roll // 2))) * block, block)
        lhs[pl.ds(at, block), :] = parts[k][...]
    w = w_ref[pl.ds(pl.multiple_of(side * cols, cols), cols), :]
    part = jnp.dot(lhs[...], w, preferred_element_type=jnp.float32)
    if not theirs:
        rest[0][...] = part
        return
    part = rest[0][...] + part
    keep_ref, send_ref = rest[1:3]
    rows = keep_ref.shape[0]
    keep_ref[...] = part[:rows]
    send_ref[...] = part[rows:].astype(send_ref.dtype)


def output(parts, w_out, before=None):
    roll = len(parts)
    block, cols = parts[0].shape
    width = w_out.shape[1]
    rows = roll * block
    vmem = pl.BlockSpec(memory_space=pltpu.VMEM)
    theirs = before is not None
    if theirs:
        shapes = [
            jax.ShapeDtypeStruct((rows // 2, width), jnp.float32),
            jax.ShapeDtypeStruct((rows // 2, width), jnp.bfloat16),
        ]
    else:
        shapes = jax.ShapeDtypeStruct((rows, width), jnp.float32)
    return pl.pallas_call(
        functools.partial(output_kernel, roll, theirs),
        in_specs=[vmem] * (roll + 1 + theirs),
        out_specs=[vmem, vmem] if theirs else vmem,
        scratch_shapes=[pltpu.VMEM((rows, cols), jnp.bfloat16)],
        out_shape=shapes,
        compiler_params=pltpu.CompilerParams(vmem_limit_bytes=16 << 20),
        cost_estimate=pl.CostEstimate(
            flops=2 * rows * cols * width, bytes_accessed=2 * cols * width, transcendentals=0
        ),
        name="output_theirs" if theirs else "output_mine",
    )(*parts, w_out, *((before,) if theirs else ()))


def fast_body(
    hidden,
    w_query,
    w_key,
    w_value,
    b_query,
    b_key,
    b_value,
    w_out,
    prefix_keys,
    prefix_values,
    suffix_keys,
    suffix_values,
    suffix_lengths,
    prompt_of,
):
    roll = lax.axis_size("roll")
    kv_heads = w_key.shape[1] // HD
    group = w_query.shape[1] // w_key.shape[1]
    kh = kv_heads // 2
    per = suffix_keys.shape[0]
    block = hidden.shape[0] // roll
    guess = block // per
    scale = 1.0 / math.sqrt(HD)

    def across(x):
        return lax.ppermute(x, "seq", [(0, 1), (1, 0)])

    def hop(x, k):
        return lax.ppermute(x, "roll", [(n, n ^ k) for n in range(roll)])

    def hops(pick):
        sent = {k: hop(pick(k), k) for k in reversed(range(1, roll))}
        return [sent[k] for k in range(1, roll)]

    send, keep = project(hidden, w_query, w_key, w_value, roll, kh)
    got = across(send)
    terms = [keep[k] + got[k] for k in range(roll)]
    if roll == 4:
        relayed = hop(terms[3], 1)
        near = hop(terms[1], 1)
        sums = [terms[0], near, hop(terms[2] + relayed, 2)]
    else:
        sums = [terms[0]] + hops(lambda k: terms[k])
    caches = (suffix_keys, suffix_values, prefix_keys, prefix_values)
    _, small = lax.optimization_barrier(
        (terms[0], (suffix_lengths, b_query, b_key, b_value, *caches))
    )
    caches = small[4:]

    sk_got, sv_got, pk_got, pv_got = [across(x) for x in caches]
    sk_own, sv_own, pk_own, pv_own = fetch(caches)

    row_ids = jnp.arange(hidden.shape[0], dtype=jnp.int32)
    prefix_total = prefix_keys.shape[1] * roll * 2
    positions = (prefix_total + lookup(small[0], row_ids // guess) + row_ids % guess).astype(jnp.float32)
    half = HD // 2
    steps = jnp.arange(half).astype(jnp.float32) * (2.0 / HD)
    freqs = jnp.exp(-math.log(ROPE_BASE) * steps)
    angles = positions[:, None] * freqs[None, :]
    cosine = jnp.cos(angles)
    sine = jnp.sin(angles)
    cosine = jnp.concatenate([cosine, cosine], axis=-1)
    sine = jnp.concatenate([-sine, sine], axis=-1)
    biases = [b[None, :] for b in small[1:4]]

    q, k_new, v_new = finish(sums, biases, cosine, sine, per)
    queries = [q] + hops(lambda k: q)
    own = own_attention(
        suffix_lengths, q, k_new, v_new, sk_own, sk_got, sv_own, sv_got, scale, guess
    )
    own, packed = prefix_attention(
        prompt_of, queries, pk_own, pk_got, pv_own, pv_got, own, scale
    )
    packed = hops(lambda k: packed[k - 1])
    share = merge(own, packed, group)
    mine = [share] + hops(lambda k: share)
    theirs = []
    for m in mine:
        theirs.append(across(m))
    kept, sent = output(theirs, w_out, output(mine, w_out))
    arrived = lax.ppermute(sent, "tp", [(0, 1), (1, 0)])
    return (kept + arrived.astype(jnp.float32)).astype(jnp.bfloat16)


def body(*arrays):
    hidden, w_key, prompt_of, suffix_keys = arrays[0], arrays[2], arrays[13], arrays[10]
    roll = lax.axis_size("roll")
    block = hidden.shape[0] // roll
    fits = (
        lax.axis_size("seq") == 2
        and lax.axis_size("tp") == 2
        and roll & (roll - 1) == 0
        and (w_key.shape[1] // HD) % 2 == 0
        and block % 16 == 0
        and block == suffix_keys.shape[0] * GUESS
        and 3 * suffix_keys.shape[0] * (w_key.shape[1] // HD) <= 2 * STATS
        and 2 * GUESS * (arrays[1].shape[1] // w_key.shape[1]) == HD
        and prompt_of.shape[0] % arrays[8].shape[0] == 0
    )
    if not fits:
        return general_body(*arrays)
    return fast_body(*arrays)


def solution(mesh):
    return jax.shard_map(
        body,
        mesh=mesh,
        in_specs=(
            P("groups", ("roll", "seq")),
            P(("roll", "seq"), "tp"),
            P(("roll", "seq"), "tp"),
            P(("roll", "seq"), "tp"),
            P("tp"),
            P("tp"),
            P("tp"),
            P("tp", ("roll", "seq")),
            P("groups", ("roll", "seq"), "tp"),
            P("groups", ("roll", "seq"), "tp"),
            P(("groups", "roll"), "seq", "tp"),
            P(("groups", "roll"), "seq", "tp"),
            P("groups"),
            P("groups"),
        ),
        out_specs=P(("groups", "tp"), ("roll", "seq")),
        check_vma=False,
    )
```
